32 devices in a mesh: comp: 4 (over y, x), tile: 8 (over z, core).
Axes of the slice: x: 2, y: 2, z: 4, core: 2. Of those that a mesh axis runs over, the one named last changes fastest.
Arguments:
- atmos_state: float32 [32, 128, 128], P('comp', 'tile'), may hold values from -6 to 6
- wind_field: bfloat16 [2, 32, 128, 128], P(None, 'comp', 'tile'), may hold values from -5 to 5
- ocean_height: float32 [128, 1024], P('comp', 'tile'), may hold values from -6 to 6
- ocean_potential: float32 [128, 1024], P('comp', 'tile'), may hold values from -6 to 6
- ocean_neighbors: int32 [6, 128, 1024], P(None, 'comp', 'tile'), may hold values from 0 to 4419, as said below
- ocean_coupling: float32 [6, 128, 1024], P(None, 'comp', 'tile'), may hold values from 0.1 to 0.5
- downward_source: int32 [4, 64, 1024], P('comp', 'tile'), may hold values from 0 to 127, as said below
- downward_target: int32 [4, 64, 1024], P('comp', 'tile'), may hold values from 0 to 4095, as said below
- downward_weight: float32 [4, 64, 1024], P('comp', 'tile'), may hold values from 0.3 to 1.2
- upward_source: int32 [4, 64, 1024], P('comp', 'tile'), may hold values from 0 to 4095, as said below
- upward_target: int32 [4, 64, 1024], P('comp', 'tile'), may hold values from 0 to 127, as said below
- upward_weight: float32 [4, 64, 1024], P('comp', 'tile'), may hold values from 0.05 to 0.3
Outputs:
- atmos_out: float32 [32, 128, 128], P('comp', 'tile')
- height_out: float32 [128, 1024], P('comp', 'tile')
- potential_out: float32 [128, 1024], P('comp', 'tile')
- surface_flux: float32 [32, 128], P('comp', 'tile')
The draws below stay inside these ranges and needn't reach their ends.
Inputs may be any that keep to these rules, and one draw needn't show every extreme that they name: `ocean_neighbors`: the six entries of a cell are distinct and name the four cells beside it along the two dimensions and one of the two diagonal pairs. `downward_source`: within a row of devices the ocean's blocks are laid out differently from the atmosphere's, so the surface under one ocean block is spread over all devices of the row; band p of a device's local points (flat order, p * 8 * 2 onward, 16 of them) lies over row-peer p. Entries for peer p name points of band p. `downward_target`: entries from peer p name ocean cells of band p of the receiving device's cells (flat order, 512 of them from p * 32 * 16). `upward_source`: entries for peer p name ocean cells of band p of the sending device's cells (flat order, 512 of them from p * 32 * 16). `upward_target`: entries from peer p name surface points of band p of the receiving device's points (flat order, 16 of them from p * 8 * 2).
All inputs are finite; a program needn't handle non-finite values.
Results may differ from the reference program's by a relative error of at most 0.0003.
Values sent between devices are 32-bit elements; how exact they have to be, the bound alone decides.
No kernel may reach another device: no remote copies, remote signals or barrier semaphores. Data moves between devices by JAX's collectives and lax.ppermute only.
A program may use at most 64 MiB of HBM per device.

```python
import jax
import jax.numpy as jnp
import numpy as np
from jax import lax

NP = 4
LEV = 128
OX = 32
OY = 128
SUBSTEPS = 2
SUBCYCLES = 8
AX = 8
AY = 16
NXA = 32
NYA = 128
OXT = 128
OYT = 1024
SLOT = 1024
N_COMP = 4
N_TILE = 8


def draw_ocean_neighbors(key, part):
    choose = jax.random.randint(jax.random.fold_in(key, 17), (OXT, OYT), 0, 2)
    row_local = jnp.arange(OXT, dtype=jnp.int32)[:, None] % OX
    col_local = jnp.arange(OYT, dtype=jnp.int32)[None, :] % OY
    corner = (row_local == 0) & (col_local == 0) | (row_local == OX - 1) & (col_local == OY - 1)
    choose = jnp.where(corner, 0, choose)
    diagonal = 1 - 2 * choose
    zeros_grid = jnp.zeros((OXT, OYT), jnp.int32)
    offset_row = jnp.stack([zeros_grid - 1, zeros_grid + 1, zeros_grid, zeros_grid, zeros_grid + 1, zeros_grid - 1])
    offset_col = jnp.stack([zeros_grid, zeros_grid, zeros_grid - 1, zeros_grid + 1, diagonal, 0 - diagonal])
    flat_index = (row_local[None] + 1 + offset_row) * (OY + 2) + (col_local[None] + 1 + offset_col)
    return flat_index.astype(jnp.int32)


def banded_table(key, extent):
    band = extent // N_TILE
    peer = (jnp.arange(N_TILE * N_TILE, dtype=jnp.int32) % N_TILE)[None, :, None]
    within = jax.random.randint(key, (N_COMP, N_TILE * N_TILE, SLOT), 0, band)
    return (peer * band + within).astype(jnp.int32)


def draw_downward_source(key, part):
    return banded_table(jax.random.fold_in(key, 31), AX * AY)


def draw_downward_target(key, part):
    return banded_table(jax.random.fold_in(key, 37), OX * OY)


def draw_upward_source(key, part):
    return banded_table(jax.random.fold_in(key, 41), OX * OY)


def draw_upward_target(key, part):
    return banded_table(jax.random.fold_in(key, 43), AX * AY)


def block_levels(rng, shape, cuts, low, high):
    level = 1.0
    for axis_at, parts in cuts:
        steps = jax.random.uniform(jax.random.fold_in(jax.random.fold_in(rng, 6), axis_at), (parts,), jnp.float32, low / len(cuts), high / len(cuts))
        level = level * jnp.repeat(jnp.exp(steps), shape[axis_at] // parts).reshape((-1,) + (1,) * (len(shape) - 1 - axis_at))
    return level


def scatter_about(own_key, shape, width, limit, split=(), kind=jnp.bfloat16):
    values = jax.random.normal(own_key, shape, jnp.float32) * width
    if len(split) > 0:
        values = block_levels(own_key, shape, split, -0.22, 0.18) * values
    return jnp.clip(values, min=-limit, max=limit).astype(kind)


def setup_inputs(seed: int = 0) -> dict:
    keys = jax.random.split(jax.random.key(seed), 13)
    return {
        "atmos_state": scatter_about(keys[0], (NXA, NYA, LEV), 1.0, 6.0, ((0, 4), (1, 8)), jnp.float32),
        "wind_field": scatter_about(keys[1], (2, NXA, NYA, LEV), 1.0, 5.0, ((1, 4), (2, 8))),
        "ocean_height": scatter_about(keys[2], (OXT, OYT), 1.0, 6.0, ((0, 4), (1, 8)), jnp.float32),
        "ocean_potential": scatter_about(keys[3], (OXT, OYT), 1.0, 6.0, ((0, 4), (1, 8)), jnp.float32),
        "ocean_neighbors": draw_ocean_neighbors(jax.random.fold_in(keys[12], 71), 0),
        "ocean_coupling": jnp.clip(0.1 + 0.4 * jax.random.uniform(keys[5], (6, OXT, OYT), jnp.float32) ** block_levels(keys[5], (6, OXT, OYT), ((1, 4), (2, 8)), -0.2, 0.2), 0.1, 0.5),
        "downward_source": draw_downward_source(jax.random.fold_in(keys[12], 71), 0),
        "downward_target": draw_downward_target(jax.random.fold_in(keys[12], 71), 0),
        "downward_weight": jnp.clip(0.3 + 0.90000004 * jax.random.uniform(keys[8], (N_COMP, N_TILE * N_TILE, SLOT), jnp.float32) ** block_levels(keys[8], (N_COMP, N_TILE * N_TILE, SLOT), ((0, 4), (1, 8)), -0.2, 0.2), 0.3, 1.2),
        "upward_source": draw_upward_source(jax.random.fold_in(keys[12], 71), 0),
        "upward_target": draw_upward_target(jax.random.fold_in(keys[12], 71), 0),
        "upward_weight": jnp.clip(0.05 + 0.25 * jax.random.uniform(keys[11], (N_COMP, N_TILE * N_TILE, SLOT), jnp.float32) ** block_levels(keys[11], (N_COMP, N_TILE * N_TILE, SLOT), ((0, 4), (1, 8)), -0.2, 0.2), 0.05, 0.3),
    }


atmos_step = 0.05
viscosity = 0.05
ocean_step = 0.2
wave_speed = 1.0
friction = 0.05

def gll_derivative():
    points = np.array([-1.0, -1.0 / np.sqrt(5.0), 1.0 / np.sqrt(5.0), 1.0])
    weights = np.array([1.0 / np.prod([points[j] - points[k] for k in range(4) if k != j]) for j in range(4)])
    matrix = np.zeros((4, 4))
    for i in range(4):
        for j in range(4):
            if i != j:
                matrix[i, j] = weights[j] / weights[i] / (points[i] - points[j])
        matrix[i, i] = -np.sum(matrix[i])
    return matrix

def along_first(values, matrix):
    extent_rows, extent_cols, levels = values.shape
    shaped = values.reshape(extent_rows // NP, NP, extent_cols, levels)
    result = jnp.einsum('ik,ekyl->eiyl', matrix, shaped, precision=lax.Precision.HIGHEST)
    return result.reshape(extent_rows, extent_cols, levels)

def along_second(values, matrix):
    extent_rows, extent_cols, levels = values.shape
    shaped = values.reshape(extent_rows, extent_cols // NP, NP, levels)
    result = jnp.einsum('ik,xekl->xeil', matrix, shaped, precision=lax.Precision.HIGHEST)
    return result.reshape(extent_rows, extent_cols, levels)

def tendency(atmos, wind_east, wind_north):
    first_order = gll_derivative()
    second_order = jnp.asarray(first_order @ first_order, jnp.float32)
    first_order = jnp.asarray(first_order, jnp.float32)
    slope_east = along_first(atmos, first_order)
    slope_north = along_second(atmos, first_order)
    curvature = along_first(atmos, second_order) + along_second(atmos, second_order)
    return viscosity * curvature - (wind_east * slope_east + wind_north * slope_north)

def pair_mean(values, after, before, axis):
    length = values.shape[axis]
    extent = [1] * values.ndim
    extent[axis] = length
    position = (jnp.arange(length, dtype=jnp.int32) % NP).reshape(extent)
    return jnp.where(position == NP - 1, 0.5 * (values + after), jnp.where(position == 0, 0.5 * (values + before), values))

def assemble(tendency_field):
    across = pair_mean(tendency_field, jnp.roll(tendency_field, -1, 0), jnp.roll(tendency_field, 1, 0), 0)
    return pair_mean(across, jnp.roll(across, -1, 1), jnp.roll(across, 1, 1), 1)

def stencil(neighbors, coupling):
    extent_rows, extent_cols = (neighbors.shape[1], neighbors.shape[2])
    row_local = (jnp.arange(extent_rows, dtype=jnp.int32) % OX)[None, :, None]
    col_local = (jnp.arange(extent_cols, dtype=jnp.int32) % OY)[None, None, :]
    offset_row = neighbors // (OY + 2) - 1 - row_local
    offset_col = neighbors % (OY + 2) - 1 - col_local
    offset_code = (offset_row + 1) * 3 + offset_col + 1
    layers = [lax.optimization_barrier(jnp.sum(jnp.where(offset_code == o, coupling, 0.0), axis=0)) for o in range(9)]
    layers[4] = layers[4] - lax.optimization_barrier(jnp.sum(coupling, axis=0))
    return jnp.stack(layers)

def spread(weights_nine, values):
    summed = jnp.zeros_like(values)
    for o in range(9):
        summed = summed + weights_nine[o] * jnp.roll(values, (1 - o // 3, 1 - o % 3), (0, 1))
    return summed

def to_blocks(values, rows_dev, cols_dev):
    shaped = values.reshape(N_COMP, rows_dev, N_TILE, cols_dev).transpose(0, 2, 1, 3)
    return shaped.reshape(N_COMP, N_TILE, rows_dev * cols_dev)

def from_blocks(blocks, rows_dev, cols_dev):
    shaped = blocks.reshape(N_COMP, N_TILE, rows_dev, cols_dev).transpose(0, 2, 1, 3)
    return shaped.reshape(N_COMP * rows_dev, N_TILE * cols_dev)

def remap(blocks, source, target, weight, cell_count):
    picked = jnp.take_along_axis(blocks, source.reshape(N_COMP, N_TILE, N_TILE * SLOT), axis=2)
    picked = picked.reshape(N_COMP, N_TILE, N_TILE, SLOT).transpose(0, 2, 1, 3)
    products = weight.reshape(N_COMP, N_TILE, N_TILE, SLOT) * picked
    device = jnp.arange(N_COMP * N_TILE, dtype=jnp.int32).reshape(N_COMP, N_TILE, 1, 1)
    flat_index = device * cell_count + target.reshape(N_COMP, N_TILE, N_TILE, SLOT)
    summed = jax.ops.segment_sum(products.reshape(-1), flat_index.reshape(-1), num_segments=N_COMP * N_TILE * cell_count)
    return summed.reshape(N_COMP, N_TILE, cell_count)

def reference(atmos_state, wind_field, ocean_height, ocean_potential, ocean_neighbors, ocean_coupling, downward_source, downward_target, downward_weight, upward_source, upward_target, upward_weight):
    atmos = atmos_state
    wind_east = wind_field[0].astype(jnp.float32)
    wind_north = wind_field[1].astype(jnp.float32)
    for substep in range(SUBSTEPS):
        tendency_field = tendency(atmos, wind_east, wind_north)
        atmos = atmos + atmos_step * assemble(tendency_field)
    surface = to_blocks(atmos[:, :, LEV - 1], AX, AY)
    forcing = from_blocks(remap(surface, downward_source, downward_target, downward_weight, OX * OY), OX, OY)
    weights_nine = stencil(ocean_neighbors, ocean_coupling)
    height = ocean_height
    potential = ocean_potential
    for substep in range(SUBCYCLES):
        potential = (1.0 - friction) * potential + ocean_step * (wave_speed * height + forcing)
        height = height + ocean_step * spread(weights_nine, potential)
    cells = to_blocks(height, OX, OY)
    surface_flux = from_blocks(remap(cells, upward_source, upward_target, upward_weight, AX * AY), AX, AY)
    return (atmos, height, potential, surface_flux)
```

```python
import functools

import jax
import jax.numpy as jnp
import numpy as np
from jax import lax
from jax.experimental import pallas as pl
from jax.experimental.pallas import tpu as pltpu
from jax.sharding import PartitionSpec as P

NP = 4
SUBCYCLES = 8

atmos_step = 0.05
viscosity = 0.05
ocean_step = 0.2
wave_speed = 1.0
friction = 0.05

OFFSETS = [(a, b) for a in (-1, 0, 1) for b in (-1, 0, 1) if (a, b) != (0, 0)]
FIELDS = 3 + len(OFFSETS)


def gll_derivative():
    points = np.array([-1.0, -1.0 / np.sqrt(5.0), 1.0 / np.sqrt(5.0), 1.0])
    weights = np.array(
        [1.0 / np.prod([points[j] - points[k] for k in range(4) if k != j]) for j in range(4)]
    )
    matrix = np.zeros((4, 4))
    for i in range(4):
        for j in range(4):
            if i != j:
                matrix[i, j] = weights[j] / weights[i] / (points[i] - points[j])
        matrix[i, i] = -np.sum(matrix[i])
    return matrix


D1 = gll_derivative()
D2 = D1 @ D1


def band_coefficients(position, matrix):
    result = {}
    for shift in range(1 - NP, NP):
        value = jnp.zeros(position.shape, jnp.float32)
        for i in range(NP):
            if 0 <= i + shift < NP:
                value = jnp.where(position == i, float(matrix[i, i + shift]), value)
        result[shift] = value
    return result


def iota(shape, dim):
    return lax.broadcasted_iota(jnp.int32, shape, dim)


def full_specs(count):
    return [pl.BlockSpec(memory_space=pltpu.VMEM) for _ in range(count)]


def call(body, name, out_shapes, smem, args, scratch=(), flops=1000000, moved=1000000):
    return pl.pallas_call(
        body,
        name=name,
        out_shape=[jax.ShapeDtypeStruct(s, d) for s, d in out_shapes],
        in_specs=[pl.BlockSpec(memory_space=pltpu.SMEM)] * len(smem) + full_specs(len(args)),
        out_specs=full_specs(len(out_shapes)),
        scratch_shapes=list(scratch),
        compiler_params=pltpu.CompilerParams(vmem_limit_bytes=16 * 1024 * 1024),
        cost_estimate=pl.CostEstimate(flops=flops, bytes_accessed=moved, transcendentals=0),
    )(*smem, *args)


def column_shift(row, shift):
    extent, levels = row.shape
    tiles = row.reshape(extent // 8, 8, levels)
    return pltpu.roll(tiles, (-shift) % 8, 1).reshape(extent, levels)


def second_terms(row, first_c, second_c):
    slope = first_c[0] * row
    curve = second_c[0] * row
    for shift in range(1 - NP, NP):
        if shift:
            moved = column_shift(row, shift)
            slope = slope + first_c[shift] * moved
            curve = curve + second_c[shift] * moved
    return slope, curve


def row_rate(element, position, wind_east, wind_north, first_c, second_c):
    slope_east = sum(float(D1[position, k]) * element[k] for k in range(NP))
    curve_east = sum(float(D2[position, k]) * element[k] for k in range(NP))
    slope_north, curve_north = second_terms(element[position], first_c, second_c)
    return viscosity * (curve_east + curve_north) - (
        wind_east * slope_east + wind_north * slope_north
    )


def column_mean(row, left_edge, right_edge):
    extent, levels = row.shape
    at = iota((extent, levels), 0)
    after = jnp.where(at == extent - 1, right_edge, pltpu.roll(row, extent - 1, 0))
    before = jnp.where(at == 0, left_edge, pltpu.roll(row, 1, 0))
    position = at % NP
    return jnp.where(
        position == NP - 1,
        0.5 * (row + after),
        jnp.where(position == 0, 0.5 * (row + before), row),
    )


def column_coefficients(extent, levels):
    position = iota((extent, levels), 0) % NP
    return band_coefficients(position, D1), band_coefficients(position, D2)


def static_kernel(
    sizes, nbr_ref, cpl_ref, h_ref, p_ref, tgt_ref, wgt_ref, a_ref, wind_ref,
    up_ref, dn_ref, w8_ref, rate_ref,
):
    AX, AY, LEV, OX, OY, T, SLOT, H, nbh = sizes
    ks = SLOT // 128
    row = iota((OX, OY), 0)
    col = iota((OX, OY), 1)
    centre = (row + 1) * (OY + 2) + col + 1
    offset = [nbr_ref[l] - centre for l in range(6)]
    coupling = [cpl_ref[l] for l in range(6)]
    fields = [h_ref[...], p_ref[...]]
    for o, (dr, dc) in enumerate(OFFSETS):
        code = dr * (OY + 2) + dc
        layer = jnp.zeros((OX, OY), jnp.float32)
        for l in range(6):
            layer = layer + jnp.where(offset[l] == code, coupling[l], 0.0)
        w8_ref[o] = layer
        fields.append(layer)
    for f, field in enumerate(fields):
        up_ref[H * f : H * f + H, :] = field[:H]
        dn_ref[H * f : H * f + H, :] = field[OX - H :]
    base = H * len(fields)
    for ref in (tgt_ref, wgt_ref):
        table = ref[...].astype(jnp.float32)
        for k in range(ks):
            chunk = table[:, 128 * k : 128 * k + 128]
            up_ref[base : base + nbh, :] = chunk[:nbh]
            dn_ref[base : base + nbh, :] = chunk[T - nbh :]
            base += nbh
    first_c, second_c = column_coefficients(AY, LEV)
    rates = []
    for i in range(AX):
        start = i - i % NP
        element = [a_ref[start + k] for k in range(NP)]
        rates.append(
            row_rate(
                element,
                i % NP,
                wind_ref[0, i].astype(jnp.float32),
                wind_ref[1, i].astype(jnp.float32),
                first_c,
                second_c,
            )
        )
        rate_ref[i] = rates[i]
    for ref, rate_rows, state_rows, rim in (
        (up_ref, list(range(NP + 1)), list(range(NP)), 0),
        (dn_ref, list(range(AX - NP - 1, AX)), list(range(AX - NP, AX)), AX - 1),
    ):
        at = base
        for i in rate_rows:
            ref[at : at + AY, :] = rates[i]
            at += AY
        for i in state_rows:
            ref[at : at + AY, :] = a_ref[i]
            at += AY
        for n in range(2):
            ref[at : at + AY, :] = wind_ref[n, rim].astype(jnp.float32)
            at += AY


def surface_coefficients(shape, stride, matrix):
    return band_coefficients((iota(shape, 1) // stride) % NP, matrix)


def surface_steps(blocks, winds, AX, AY):
    shape = blocks[0].shape
    n = AX * AY
    lane = iota(shape, 1)
    i_at, j_at = lane // AY, lane % AY
    x1 = surface_coefficients(shape, AY, D1)
    x2 = surface_coefficients(shape, AY, D2)
    y1 = surface_coefficients(shape, 1, D1)
    y2 = surface_coefficients(shape, 1, D2)

    def lanes(v, shift):
        return pltpu.roll(v, (-shift) % n, 1) if shift % n else v

    def rate(v, east, north):
        slope_e, slope_n, curve = x1[0] * v, y1[0] * v, (x2[0] + y2[0]) * v
        for s in range(1 - NP, NP):
            if s:
                along = lanes(v, s * AY)
                slope_e = slope_e + x1[s] * along
                curve = curve + x2[s] * along
                along = lanes(v, s)
                slope_n = slope_n + y1[s] * along
                curve = curve + y2[s] * along
        return viscosity * curve - (east * slope_e + north * slope_n)

    def mean_columns(v):
        devices = shape[0]
        following = pltpu.roll(v, devices - 1, 0)
        preceding = pltpu.roll(v, 1, 0)
        after = jnp.where(j_at == AY - 1, lanes(following, 1 - AY), lanes(v, 1))
        before = jnp.where(j_at == 0, lanes(preceding, AY - 1), lanes(v, -1))
        return jnp.where(
            j_at % NP == NP - 1,
            0.5 * (v + after),
            jnp.where(j_at % NP == 0, 0.5 * (v + before), v),
        )

    def mean_rows(v, above, below):
        after = jnp.where(i_at == AX - 1, lanes(below, AY - n), lanes(v, AY))
        before = jnp.where(i_at == 0, lanes(above, n - AY), lanes(v, -AY))
        return jnp.where(
            i_at % NP == NP - 1,
            0.5 * (v + after),
            jnp.where(i_at % NP == 0, 0.5 * (v + before), v),
        )

    for substep in range(2):
        across = [mean_columns(rate(v, e, w)) for v, (e, w) in zip(blocks, winds)]
        count = len(blocks)
        blocks = [
            blocks[b]
            + atmos_step
            * mean_rows(across[b], across[max(b - 1, 0)], across[min(b + 1, count - 1)])
            for b in range(count)
        ]
    return blocks


def remap_kernel(
    sizes, where_ref, got_ref, fup_ref, fdn_ref, h_ref, p_ref, w8_ref, tgt_ref, wgt_ref,
    rate_ref, ext_ref, mean_ref, left_ref, right_ref, tgt_s, hi_s, mid_s, lo_s, row_s,
):
    AX, AY, LEV, OX, OY, T, SLOT, H, nbh = sizes
    ks = SLOT // 128
    n = AX * AY
    NB = T + 2 * nbh
    cells = OX * OY
    band = cells // T
    rb = max(1, band // OY)
    gs = max(1, OY // band)
    static_fields = FIELDS - 1

    base = H * static_fields + 2 * nbh * ks
    up_rows = [fup_ref[base + AY * k : base + AY * k + AY, :] for k in range(NP + 1)]
    dn_rows = [fdn_ref[base + AY * k : base + AY * k + AY, :] for k in range(NP + 1)]
    rates = up_rows + [rate_ref[i] for i in range(AX)] + dn_rows
    edge_left, edge_right = [], []
    for i in range(-NP, AX + NP):
        at = i + NP + 1
        if i % NP == NP - 1:
            value = 0.5 * (rates[at] + rates[at + 1])
        elif i % NP == 0:
            value = 0.5 * (rates[at] + rates[at - 1])
        else:
            value = rates[at]
        mean_ref[i + NP] = value
    rows = AX + 2 * NP
    groups = (OX + 2 * H) // 8
    left_ref[8 * groups :, :] = mean_ref[:, 0, :]
    right_ref[8 * groups :, :] = mean_ref[:, AY - 1, :]

    def slot(c, lo, hi):
        return got_ref[pl.ds(pl.multiple_of(where_ref[c] * T, T), T), lo:hi]

    blocks = [slot(2 + k, SLOT, SLOT + n) for k in range(5)]
    winds = [
        (slot(2 + k, SLOT + n, SLOT + 2 * n), slot(2 + k, SLOT + 2 * n, SLOT + 3 * n))
        for k in range(5)
    ]
    final = surface_steps(blocks, winds, AX, AY)[1:4]

    base = H * static_fields
    for k in range(ks):
        at = slice(128 * k, 128 * k + 128)
        picked = [
            jnp.take_along_axis(
                final[b], slot(3 + b, 128 * k, 128 * k + 128).astype(jnp.int32), axis=1,
                mode="promise_in_bounds",
            )
            for b in range(3)
        ]
        t_lo, w_lo = base + k * nbh, base + (ks + k) * nbh
        for lo, count, value, target, weight in (
            (0, nbh, picked[0][T - nbh :], fup_ref[t_lo : t_lo + nbh, :], fup_ref[w_lo : w_lo + nbh, :]),
            (nbh, T, picked[1], tgt_ref[:, at].astype(jnp.float32), wgt_ref[:, at]),
            (nbh + T, nbh, picked[2][:nbh], fdn_ref[t_lo : t_lo + nbh, :], fdn_ref[w_lo : w_lo + nbh, :]),
        ):
            product = weight * value
            hi = product.astype(jnp.bfloat16).astype(jnp.float32)
            rest = product - hi
            mid = rest.astype(jnp.bfloat16).astype(jnp.float32)
            target = target.astype(jnp.int32)
            tgt_s[lo : lo + count, at] = target & (OY - 1)
            row_s[lo : lo + count, at] = (target // OY) & (rb - 1)
            hi_s[lo : lo + count, at] = hi
            mid_s[lo : lo + count, at] = mid
            lo_s[lo : lo + count, at] = rest - mid

    for f in range(static_fields):
        own = h_ref[...] if f == 0 else p_ref[...] if f == 1 else w8_ref[f - 2]
        ext_ref[f, :H, :] = fup_ref[H * f : H * f + H, :]
        ext_ref[f, H : H + OX, :] = own
        ext_ref[f, H + OX :, :] = fdn_ref[H * f : H * f + H, :]

    width = gs * SLOT
    mrows = max(16, -(-3 * rb // 16) * 16)
    part = iota((mrows, SLOT), 0) // rb
    part_row = iota((mrows, SLOT), 0) % rb
    column = iota((OY, SLOT), 0)
    for g in range(NB // gs):
        total = None
        for b in range(g * gs, g * gs + gs):
            choose = jnp.where(
                part == 0,
                hi_s[b : b + 1, :],
                jnp.where(part == 1, mid_s[b : b + 1, :], jnp.where(part == 2, lo_s[b : b + 1, :], 0.0)),
            )
            left = jnp.where(row_s[b : b + 1, :] == part_row, choose, 0.0).astype(jnp.bfloat16)
            hot = jnp.where(tgt_s[b : b + 1, :] == column, 1.0, 0.0).astype(jnp.bfloat16)
            placed = lax.dot_general(
                left, hot, (((1,), (1,)), ((), ())), preferred_element_type=jnp.float32
            )
            total = placed if total is None else total + placed
        ext_ref[static_fields, g * rb : g * rb + rb, :] = (
            total[:rb] + total[rb : 2 * rb] + total[2 * rb : 3 * rb]
        )

    lane_slot = iota((8, OY), 1) // H
    for g in range(groups):
        low = jnp.zeros((8, OY), jnp.float32)
        high = jnp.zeros((8, OY), jnp.float32)
        for f in range(FIELDS):
            block = ext_ref[f, 8 * g : 8 * g + 8, :]
            here = lane_slot == f
            to_low = (H * f) % OY
            to_high = (H * f - (OY - H)) % OY
            low = jnp.where(here, pltpu.roll(block, to_low, 1) if to_low else block, low)
            high = jnp.where(here, pltpu.roll(block, to_high, 1) if to_high else block, high)
        left_ref[8 * g : 8 * g + 8, :] = low
        right_ref[8 * g : 8 * g + 8, :] = high


def ocean_kernel(
    sizes, where_ref, ext_ref, fl_ref, fr_ref, mean_ref, fup_ref, fdn_ref, a_ref, wind_ref, src_ref,
    h_out, p_out, send_ref, next_ref, mean2_ref,
):
    AX, AY, LEV, OX, OY, T, SLOT, H, nbh = sizes
    ks = SLOT // 128
    rows = OX + 2 * H
    groups = rows // 8
    lane = iota((8, OY), 1)

    def halo(f):
        parts = []
        for g in range(groups):
            from_right = fr_ref[8 * g : 8 * g + 8, :]
            from_left = fl_ref[8 * g : 8 * g + 8, :]
            sr = (-H * f) % OY
            sl = (OY - H - H * f) % OY
            from_right = pltpu.roll(from_right, sr, 1) if sr else from_right
            from_left = pltpu.roll(from_left, sl, 1) if sl else from_left
            parts.append(
                jnp.where(lane < H, from_right, jnp.where(lane >= OY - H, from_left, 0.0))
            )
        return jnp.concatenate(parts, axis=0)

    def wide(f):
        return jnp.concatenate([ext_ref[f], halo(f)], axis=1)

    height, potential = wide(0), wide(1)
    push = ocean_step * wide(FIELDS - 1)
    moved = {}
    centre = None
    for o, (dr, dc) in enumerate(OFFSETS):
        layer = ocean_step * wide(2 + o)
        centre = -layer if centre is None else centre - layer
        moved[dr, dc] = pltpu.roll(layer, dr % rows, 0) if dr else layer
    moved[0, 0] = centre
    width = 2 * OY
    for substep in range(SUBCYCLES):
        potential = (1.0 - friction) * potential + (ocean_step * wave_speed) * height + push
        shifted = {
            -1: pltpu.roll(potential, 1, 1),
            0: potential,
            1: pltpu.roll(potential, width - 1, 1),
        }
        part = {
            dr: sum(moved[dr, dc] * shifted[dc] for dc in (-1, 0, 1)) for dr in (-1, 0, 1)
        }
        height = height + part[0] + pltpu.roll(part[1], rows - 1, 0) + pltpu.roll(part[-1], 1, 0)
    final = height[H : H + OX, :OY]
    h_out[...] = final
    p_out[...] = potential[H : H + OX, :OY]

    band = OX * OY // T
    rb = max(1, band // OY)
    source = src_ref[...]
    operands = []
    for r in range(rb):
        operands.append(
            jnp.concatenate(
                [final[(q * band) // OY + r : (q * band) // OY + r + 1, :] for q in range(T)], axis=0
            )
        )
    for k in range(ks):
        index = source[:, 128 * k : 128 * k + 128]
        lanes_at = index & (OY - 1)
        row_at = (index // OY) & (rb - 1)
        value = None
        for r in range(rb):
            got = jnp.take_along_axis(operands[r], lanes_at, axis=1, mode="promise_in_bounds")
            value = got if value is None else jnp.where(row_at == r, got, value)
        for q in range(T):
            send_ref[q, AX + k : AX + k + 1, :] = value[q : q + 1, :]

    base = H * (FIELDS - 1) + 2 * nbh * ks + AY * (NP + 1)
    state = []
    for i in range(-NP, AX + NP):
        if i < 0:
            before = fup_ref[base + AY * (i + NP) : base + AY * (i + NP + 1), :]
        elif i >= AX:
            before = fdn_ref[base + AY * (i - AX) : base + AY * (i - AX + 1), :]
        else:
            before = a_ref[i]
        at = i + NP
        left = fl_ref[8 * groups + at : 8 * groups + at + 1, :]
        right = fr_ref[8 * groups + at : 8 * groups + at + 1, :]
        value = before + atmos_step * column_mean(mean_ref[at], left, right)
        state.append(value)
        if 0 <= i < AX:
            next_ref[i] = value
    base = base + AY * NP
    first_c, second_c = column_coefficients(AY, LEV)
    rates = {}
    for i in range(-1, AX + 1):
        start = i - i % NP
        element = [state[start + k + NP] for k in range(NP)]
        if i < 0:
            winds = [fup_ref[base + AY * m : base + AY * m + AY, :] for m in range(2)]
        elif i >= AX:
            winds = [fdn_ref[base + AY * m : base + AY * m + AY, :] for m in range(2)]
        else:
            winds = [wind_ref[m, i].astype(jnp.float32) for m in range(2)]
        rates[i] = row_rate(element, i % NP, winds[0], winds[1], first_c, second_c)
    for i in range(AX):
        if i % NP == NP - 1:
            value = 0.5 * (rates[i] + rates[i + 1])
        elif i % NP == 0:
            value = 0.5 * (rates[i] + rates[i - 1])
        else:
            value = rates[i]
        mean2_ref[i] = value
    left_edge = mean2_ref[:, 0, :]
    right_edge = mean2_ref[:, AY - 1, :]
    for q in range(T):
        send_ref[q, :AX, :] = jnp.where(
            where_ref[1] == q, right_edge, jnp.where(where_ref[0] == q, left_edge, 0.0)
        )


def final_kernel(
    sizes, where_ref, got_ref, next_ref, mean2_ref, tgt_ref, wgt_ref, a_out, flux_out,
):
    AX, AY, LEV, OX, OY, T, SLOT, H, nbh = sizes
    ks = SLOT // 128
    points = AX * AY // T
    left = got_ref[where_ref[0], :AX, :]
    right = got_ref[where_ref[1], :AX, :]
    for i in range(AX):
        a_out[i] = next_ref[i] + atmos_step * column_mean(
            mean2_ref[i], left[i : i + 1], right[i : i + 1]
        )
    base = iota((T, 128), 0) * points
    totals = [jnp.zeros((T, 128), jnp.float32) for _ in range(points)]
    for k in range(ks):
        value = jnp.concatenate([got_ref[q, AX + k : AX + k + 1, :] for q in range(T)], axis=0)
        product = wgt_ref[:, 128 * k : 128 * k + 128] * value
        local = tgt_ref[:, 128 * k : 128 * k + 128] - base
        for m in range(points):
            totals[m] = totals[m] + jnp.where(local == m, product, 0.0)
    for m in range(points):
        flux_out[:, m : m + 1] = jnp.sum(totals[m], axis=1, keepdims=True)


def on_device(
    C, T,
    atmos_state, wind_field, ocean_height, ocean_potential, ocean_neighbors, ocean_coupling,
    downward_source, downward_target, downward_weight, upward_source, upward_target, upward_weight,
):
    AX, AY, LEV = atmos_state.shape
    OX, OY = ocean_height.shape
    SLOT = downward_source.shape[-1]
    H = SUBCYCLES
    n = AX * AY
    band = OX * OY // T
    nbh = H * OY // band
    ks = SLOT // 128
    sizes = (AX, AY, LEV, OX, OY, T, SLOT, H, nbh)
    f32, i32 = jnp.float32, jnp.int32
    c, t = lax.axis_index("comp"), lax.axis_index("tile")
    where_at = jnp.stack(
        [(t + T - 1) % T, (t + 1) % T] + [(c + C + k) % C for k in (-2, -1, 0, 1, 2)]
    ).astype(i32)

    surface = jnp.concatenate(
        [
            atmos_state[:, :, -1].reshape(1, n),
            wind_field[0, :, :, -1].astype(f32).reshape(1, n),
            wind_field[1, :, :, -1].astype(f32).reshape(1, n),
        ],
        axis=1,
    )
    slots = jnp.concatenate(
        [
            jnp.broadcast_to(downward_source.astype(f32), (C, T, SLOT)),
            jnp.broadcast_to(surface[None], (C, T, 3 * n)),
        ],
        axis=2,
    ).reshape(C * T, SLOT + 3 * n)
    got = lax.all_to_all(slots, ("comp", "tile"), 0, 0, tiled=True)

    static_rows = H * (FIELDS - 1) + 2 * nbh * ks + AY * (2 * NP + 3)
    to_up, to_dn, w8, rate = call(
        functools.partial(static_kernel, sizes),
        "static",
        [((static_rows, 128), f32)] * 2 + [((FIELDS - 3, OX, OY), f32), ((AX, AY, LEV), f32)],
        (),
        (
            ocean_neighbors, ocean_coupling, ocean_height, ocean_potential,
            downward_target[0], downward_weight[0], atmos_state, wind_field,
        ),
    )
    forward = [(i, (i + 1) % C) for i in range(C)]
    backward = [(b, a) for a, b in forward]
    from_up = lax.ppermute(to_dn, "comp", forward)
    from_dn = lax.ppermute(to_up, "comp", backward)

    edge_rows = OX + 2 * H + AX + 2 * NP
    table = (T + 2 * nbh, SLOT)
    ext, mean, to_left, to_right = call(
        functools.partial(remap_kernel, sizes),
        "remap",
        [((FIELDS, OX + 2 * H, OY), f32), ((AX + 2 * NP, AY, LEV), f32)]
        + [((edge_rows, 128), f32)] * 2,
        (where_at,),
        (
            got, from_up, from_dn, ocean_height, ocean_potential, w8,
            downward_target[0], downward_weight[0], rate,
        ),
        scratch=[pltpu.VMEM(table, i32)] + [pltpu.VMEM(table, f32)] * 3 + [pltpu.VMEM(table, i32)],
    )
    forward = [(i, (i + 1) % T) for i in range(T)]
    backward = [(b, a) for a, b in forward]
    from_left = lax.ppermute(to_right, "tile", forward)
    from_right = lax.ppermute(to_left, "tile", backward)

    height, potential, send, state, mean2 = call(
        functools.partial(ocean_kernel, sizes),
        "ocean",
        [((OX, OY), f32)] * 2 + [((T, AX + max(8, ks), 128), f32)] + [((AX, AY, LEV), f32)] * 2,
        (where_at,),
        (
            ext, from_left, from_right, mean, from_up, from_dn, atmos_state, wind_field,
            upward_source[0],
        ),
    )
    back = lax.all_to_all(send, "tile", 0, 0, tiled=True)
    atmos, flux = call(
        functools.partial(final_kernel, sizes),
        "final",
        [((AX, AY, LEV), f32), ((T, n // T), f32)],
        (where_at,),
        (back, state, mean2, upward_target[0], upward_weight[0]),
    )
    return (atmos, height, potential, flux.reshape(AX, AY))


def solution(mesh):
    return jax.shard_map(
        functools.partial(on_device, mesh.shape["comp"], mesh.shape["tile"]),
        mesh=mesh,
        in_specs=(
            P("comp", "tile", None),
            P(None, "comp", "tile", None),
            P("comp", "tile"),
            P("comp", "tile"),
            P(None, "comp", "tile"),
            P(None, "comp", "tile"),
            P("comp", "tile", None),
            P("comp", "tile", None),
            P("comp", "tile", None),
            P("comp", "tile", None),
            P("comp", "tile", None),
            P("comp", "tile", None),
        ),
        out_specs=(
            P("comp", "tile", None),
            P("comp", "tile"),
            P("comp", "tile"),
            P("comp", "tile"),
        ),
        check_vma=False,
    )
```

```python
import functools

import jax
import jax.numpy as jnp
import numpy as np
from jax import lax
from jax.experimental import pallas as pl
from jax.experimental.pallas import tpu as pltpu
from jax.sharding import PartitionSpec as P

NP = 4
SUBCYCLES = 8

atmos_step = 0.05
viscosity = 0.05
ocean_step = 0.2
wave_speed = 1.0
friction = 0.05

OFFSETS = [(a, b) for a in (-1, 0, 1) for b in (-1, 0, 1) if (a, b) != (0, 0)]
ALL_OFFSETS = [(a, b) for a in (-1, 0, 1) for b in (-1, 0, 1)]
SENT = 2 + len(OFFSETS)
FIELDS = 3 + len(ALL_OFFSETS)
LOW = 32


def gll_derivative():
    points = np.array([-1.0, -1.0 / np.sqrt(5.0), 1.0 / np.sqrt(5.0), 1.0])
    weights = np.array(
        [1.0 / np.prod([points[j] - points[k] for k in range(4) if k != j]) for j in range(4)]
    )
    matrix = np.zeros((4, 4))
    for i in range(4):
        for j in range(4):
            if i != j:
                matrix[i, j] = weights[j] / weights[i] / (points[i] - points[j])
        matrix[i, i] = -np.sum(matrix[i])
    return matrix


D1 = gll_derivative()
D2 = D1 @ D1


def band_coefficients(position, matrix):
    result = {}
    for shift in range(1 - NP, NP):
        value = jnp.zeros(position.shape, jnp.float32)
        for i in range(NP):
            if 0 <= i + shift < NP:
                value = jnp.where(position == i, float(matrix[i, i + shift]), value)
        result[shift] = value
    return result


def iota(shape, dim):
    return lax.broadcasted_iota(jnp.int32, shape, dim)


def full_specs(count):
    return [pl.BlockSpec(memory_space=pltpu.VMEM) for _ in range(count)]


def call(body, out_shapes, args, scratch=(), raw_in=False, raw_out=0, limit=16):
    raw = pl.BlockSpec(memory_space=pltpu.HBM)
    return pl.pallas_call(
        body,
        out_shape=[jax.ShapeDtypeStruct(s, d) for s, d in out_shapes],
        in_specs=([raw] * len(args) if raw_in else full_specs(len(args))),
        out_specs=[raw] * raw_out + full_specs(len(out_shapes) - raw_out),
        scratch_shapes=list(scratch),
        compiler_params=pltpu.CompilerParams(
            vmem_limit_bytes=limit * 1024 * 1024 if limit else None
        ),
        cost_estimate=pl.CostEstimate(
            flops=1000000, bytes_accessed=1000000, transcendentals=0
        ),
    )(*args)


def column_shift(row, shift):
    extent, levels = row.shape
    tiles = row.reshape(extent // 8, 8, levels)
    return pltpu.roll(tiles, (-shift) % 8, 1).reshape(extent, levels)


def second_terms(row, first_c, second_c):
    slope = first_c[0] * row
    curve = second_c[0] * row
    for shift in range(1 - NP, NP):
        if shift:
            moved = column_shift(row, shift)
            slope = slope + first_c[shift] * moved
            curve = curve + second_c[shift] * moved
    return slope, curve


def row_rate(element, position, wind_east, wind_north, first_c, second_c):
    slope_east = sum(float(D1[position, k]) * element[k] for k in range(NP))
    curve_east = sum(float(D2[position, k]) * element[k] for k in range(NP))
    slope_north, curve_north = second_terms(element[position], first_c, second_c)
    return viscosity * (curve_east + curve_north) - (
        wind_east * slope_east + wind_north * slope_north
    )


def column_mean(row, left_edge, right_edge):
    extent, levels = row.shape
    at = iota((extent, levels), 0)
    after = jnp.where(at == extent - 1, right_edge, pltpu.roll(row, extent - 1, 0))
    before = jnp.where(at == 0, left_edge, pltpu.roll(row, 1, 0))
    position = at % NP
    return jnp.where(
        position == NP - 1,
        0.5 * (row + after),
        jnp.where(position == 0, 0.5 * (row + before), row),
    )


def column_coefficients(extent, levels):
    position = iota((extent, levels), 0) % NP
    return band_coefficients(position, D1), band_coefficients(position, D2)


def front_kernel(sizes, C, *refs):
    AX, AY, LEV, OX, OY, T, SLOT, H, nbh = sizes
    ks = SLOT // 128
    n = AX * AY
    inputs, outputs, held, made, sems = refs[:9], refs[9:14], refs[14:23], refs[23:28], refs[28]
    loads = [pltpu.make_async_copy(inputs[k], held[k], sems.at[k]) for k in range(9)]
    stores = [pltpu.make_async_copy(made[k], outputs[k], sems.at[9 + k]) for k in range(5)]
    for copy in loads:
        copy.start()
    src_ref, a_ref, wind_ref, nbr_ref, cpl_ref, h_ref, p_ref, tgt_ref, wgt_ref = held
    slots_ref, first_ref, second_ref, w8_ref, rate_ref = made
    for copy in loads[:3]:
        copy.wait()
    source = src_ref[0].astype(jnp.float32)
    surface = [
        jnp.transpose(v.astype(jnp.float32).reshape(n, LEV))[LEV - 1 :, :]
        for v in (a_ref[...], wind_ref[0], wind_ref[1])
    ]

    def spread(c, carry):
        for q in range(T):
            at = c * T + q
            slots_ref[at, :, :SLOT] = source[q : q + 1, :]
            for m in range(3):
                slots_ref[at, :, SLOT + n * m : SLOT + n * m + n] = surface[m]
        return carry

    if C <= 4:
        for c in range(C):
            spread(c, 0)
    else:
        lax.fori_loop(0, C, spread, 0)
    stores[0].start()

    even = parity("comp") == 0

    def put(at, to_up, to_dn):
        rows = slice(at, at + to_up.shape[0])
        first_ref[rows, :] = jnp.where(even, to_dn, to_up)
        second_ref[rows, :] = jnp.where(even, to_up, to_dn)

    first_c, second_c = column_coefficients(AY, LEV)
    rates = []
    for i in range(AX):
        start = i - i % NP
        element = [a_ref[start + k] for k in range(NP)]
        rates.append(
            row_rate(
                element,
                i % NP,
                wind_ref[0, i].astype(jnp.float32),
                wind_ref[1, i].astype(jnp.float32),
                first_c,
                second_c,
            )
        )
        rate_ref[i] = rates[i]
    stores[4].start()
    at = H * SENT + 2 * nbh * ks
    for k in range(NP + 1):
        put(at, rates[k], rates[AX - NP - 1 + k])
        at += AY
    for k in range(NP):
        put(at, a_ref[k], a_ref[AX - NP + k])
        at += AY
    for m in range(2):
        put(at, wind_ref[m, 0].astype(jnp.float32), wind_ref[m, AX - 1].astype(jnp.float32))
        at += AY

    for copy in loads[3:]:
        copy.wait()
    centre = (iota((OX, OY), 0) + 1) * (OY + 2) + iota((OX, OY), 1) + 1
    offset = [nbr_ref[l] - centre for l in range(6)]
    coupling = [cpl_ref[l] for l in range(6)]
    fields = [h_ref[...], p_ref[...]]
    for o, (dr, dc) in enumerate(OFFSETS):
        code = dr * (OY + 2) + dc
        layer = jnp.zeros((OX, OY), jnp.float32)
        for l in range(6):
            layer = layer + jnp.where(offset[l] == code, coupling[l], 0.0)
        w8_ref[o] = layer
        fields.append(layer)
    stores[3].start()
    for f, field in enumerate(fields):
        put(H * f, field[:H], field[OX - H :])
    at = H * SENT
    for ref in (tgt_ref, wgt_ref):
        table = ref[0].astype(jnp.float32)
        for k in range(ks):
            chunk = table[:, 128 * k : 128 * k + 128]
            put(at, chunk[:nbh], chunk[T - nbh :])
            at += nbh
    stores[1].start()
    stores[2].start()
    for copy in stores:
        copy.wait()


def parity(axis):
    return lax.rem(lax.axis_index(axis), 2)


def beside(count, step):
    return lax.rem(lax.axis_index("tile") + step + count, count)


def chosen(flag, one, other):
    return lambda lo, hi: jnp.where(flag, one[lo:hi, :], other[lo:hi, :])


def surface_coefficients(shape, stride, matrix):
    return band_coefficients((iota(shape, 1) // stride) % NP, matrix)


def surface_steps(blocks, winds, AX, AY):
    shape = blocks[0].shape
    n = AX * AY
    lane = iota(shape, 1)
    i_at, j_at = lane // AY, lane % AY
    x1 = surface_coefficients(shape, AY, D1)
    x2 = surface_coefficients(shape, AY, D2)
    y1 = surface_coefficients(shape, 1, D1)
    y2 = surface_coefficients(shape, 1, D2)

    def lanes(v, shift):
        return pltpu.roll(v, (-shift) % n, 1) if shift % n else v

    def rate(v, east, north):
        slope_e, slope_n, curve = x1[0] * v, y1[0] * v, (x2[0] + y2[0]) * v
        for s in range(1 - NP, NP):
            if s:
                along = lanes(v, s * AY)
                slope_e = slope_e + x1[s] * along
                curve = curve + x2[s] * along
                along = lanes(v, s)
                slope_n = slope_n + y1[s] * along
                curve = curve + y2[s] * along
        return viscosity * curve - (east * slope_e + north * slope_n)

    def mean_columns(v):
        devices = shape[0]
        following = pltpu.roll(v, devices - 1, 0)
        preceding = pltpu.roll(v, 1, 0)
        after = jnp.where(j_at == AY - 1, lanes(following, 1 - AY), lanes(v, 1))
        before = jnp.where(j_at == 0, lanes(preceding, AY - 1), lanes(v, -1))
        return jnp.where(
            j_at % NP == NP - 1,
            0.5 * (v + after),
            jnp.where(j_at % NP == 0, 0.5 * (v + before), v),
        )

    def mean_rows(v, above, below):
        after = jnp.where(i_at == AX - 1, lanes(below, AY - n), lanes(v, AY))
        before = jnp.where(i_at == 0, lanes(above, n - AY), lanes(v, -AY))
        return jnp.where(
            i_at % NP == NP - 1,
            0.5 * (v + after),
            jnp.where(i_at % NP == 0, 0.5 * (v + before), v),
        )

    for _ in range(2):
        across = [mean_columns(rate(v, e, w)) for v, (e, w) in zip(blocks, winds)]
        count = len(blocks)
        blocks = [
            blocks[b]
            + atmos_step
            * mean_rows(across[b], across[max(b - 1, 0)], across[min(b + 1, count - 1)])
            for b in range(count)
        ]
    return blocks


def prepare_kernel(
    sizes, first_ref, second_ref, h_ref, p_ref, w8_ref, tgt_ref, wgt_ref, rate_ref,
    ext_ref, mean_ref, left_ref, right_ref, high_ref, low_ref, weight_ref,
):
    AX, AY, _, OX, OY, T, SLOT, H, nbh = sizes
    ks = SLOT // 128
    band = OX * OY // T
    static_fields = FIELDS - 1

    even = parity("comp") == 0
    from_up = chosen(even, second_ref, first_ref)
    from_dn = chosen(even, first_ref, second_ref)

    base = H * SENT + 2 * nbh * ks
    up_rows = [from_up(base + AY * k, base + AY * k + AY) for k in range(NP + 1)]
    dn_rows = [from_dn(base + AY * k, base + AY * k + AY) for k in range(NP + 1)]
    rates = up_rows + [rate_ref[i] for i in range(AX)] + dn_rows
    for i in range(-NP, AX + NP):
        at = i + NP + 1
        if i % NP == NP - 1:
            value = 0.5 * (rates[at] + rates[at + 1])
        elif i % NP == 0:
            value = 0.5 * (rates[at] + rates[at - 1])
        else:
            value = rates[at]
        mean_ref[i + NP] = value
    groups = (OX + 2 * H) // 8
    left_ref[8 * groups :, :] = mean_ref[:, 0, :]
    right_ref[8 * groups :, :] = mean_ref[:, AY - 1, :]

    base = H * SENT
    for k in range(ks):
        at = slice(128 * k, 128 * k + 128)
        t_lo, w_lo = base + k * nbh, base + (ks + k) * nbh
        for lo, count, target, weight in (
            (0, nbh, from_up(t_lo, t_lo + nbh), from_up(w_lo, w_lo + nbh)),
            (nbh, T, tgt_ref[0, :, at], wgt_ref[0, :, at]),
            (nbh + T, nbh, from_dn(t_lo, t_lo + nbh), from_dn(w_lo, w_lo + nbh)),
        ):
            target = target.astype(jnp.int32)
            weight_ref[lo : lo + count, at] = weight
            high_ref[lo : lo + count, at] = (target & (band - 1)) // LOW
            low_ref[lo : lo + count, at] = target & (LOW - 1)

    rows = OX + 2 * H

    def extended(f):
        own = h_ref[...] if f == 0 else p_ref[...] if f == 1 else w8_ref[f - 2]
        return jnp.concatenate(
            [from_up(H * f, H * f + H), own, from_dn(H * f, H * f + H)], axis=0
        )

    ext_ref[0] = extended(0)
    ext_ref[1] = extended(1)
    layers = {d: ocean_step * extended(2 + o) for o, d in enumerate(OFFSETS)}
    layers[0, 0] = -sum(layers[d] for d in OFFSETS)
    for o, d in enumerate(ALL_OFFSETS):
        ext_ref[2 + o] = pltpu.roll(layers[d], d[0] % rows, 0) if d[0] else layers[d]
    lane_slot = iota((8, OY), 1) // H
    for g in range(groups):
        low = jnp.zeros((8, OY), jnp.float32)
        high = jnp.zeros((8, OY), jnp.float32)
        for f in range(static_fields):
            block = ext_ref[f, 8 * g : 8 * g + 8, :]
            here = lane_slot == f
            low = jnp.where(here, spin(block, H * f), low)
            high = jnp.where(here, spin(block, H * f - (OY - H)), high)
        left_ref[8 * g : 8 * g + 8, :] = low
        right_ref[8 * g : 8 * g + 8, :] = high


def spin(value, shift):
    shift = shift % value.shape[1]
    return pltpu.roll(value, shift, 1) if shift else value


def remap_kernel(
    sizes, C, got_ref, high_ref, low_ref, weight_ref, left_in, right_in,
    force_ref, first_ref, second_ref, hi_s, mid_s, lo_s, placed_s,
):
    AX, AY, _, OX, OY, T, SLOT, H, nbh = sizes
    ks = SLOT // 128
    n = AX * AY
    NB = T + 2 * nbh
    band = OX * OY // T
    groups = (OX + 2 * H) // 8

    def row_of(k):
        return lax.rem(lax.axis_index("comp") + (k - 2) + C, C)

    def slot(c, lo, hi):
        return got_ref[pl.ds(pl.multiple_of(row_of(c) * T, T), T), lo:hi]

    blocks = [slot(k, SLOT, SLOT + n) for k in range(5)]
    winds = [
        (slot(k, SLOT + n, SLOT + 2 * n), slot(k, SLOT + 2 * n, SLOT + 3 * n))
        for k in range(5)
    ]
    final = surface_steps(blocks, winds, AX, AY)[1:4]

    for k in range(ks):
        at = slice(128 * k, 128 * k + 128)
        picked = [
            jnp.take_along_axis(
                final[b], slot(1 + b, 128 * k, 128 * k + 128).astype(jnp.int32), axis=1,
                mode="promise_in_bounds",
            )
            for b in range(3)
        ]
        for lo, count, value in (
            (0, nbh, picked[0][T - nbh :]),
            (nbh, T, picked[1]),
            (nbh + T, nbh, picked[2][:nbh]),
        ):
            product = weight_ref[lo : lo + count, at] * value
            hi = product.astype(jnp.bfloat16).astype(jnp.float32)
            rest = product - hi
            mid = rest.astype(jnp.bfloat16).astype(jnp.float32)
            hi_s[lo : lo + count, at] = hi
            mid_s[lo : lo + count, at] = mid
            lo_s[lo : lo + count, at] = rest - mid

    count = band // LOW
    high_at = iota((count, SLOT), 0)
    low_at = iota((LOW, SLOT), 0)
    for b in range(NB):
        row = slice(b, b + 1)
        chosen = high_ref[row, :] == high_at
        left = jnp.concatenate(
            [jnp.where(chosen, ref[row, :], 0.0) for ref in (hi_s, mid_s, lo_s)], axis=0
        ).astype(jnp.bfloat16)
        hot = jnp.where(low_ref[row, :] == low_at, 1.0, 0.0).astype(jnp.bfloat16)
        placed = lax.dot_general(
            left, hot, (((1,), (1,)), ((), ())), preferred_element_type=jnp.float32
        )
        placed_s[count * b : count * b + count, :LOW] = (
            placed[:count] + placed[count : 2 * count] + placed[2 * count :]
        )
    pieces = OY // LOW
    lane_piece = iota((OX + 2 * H, OY), 1) // LOW
    force = None
    for q in range(pieces):
        piece = spin(placed_s[pl.ds(q, OX + 2 * H, stride=pieces), :], LOW * q)
        force = piece if force is None else jnp.where(lane_piece == q, piece, force)
    force_ref[...] = force

    f = FIELDS - 1
    here = iota((8, OY), 1) // H == f
    even = parity("tile") == 0

    def put(rows, to_left, to_right):
        first_ref[rows, :] = jnp.where(even, to_right, to_left)
        second_ref[rows, :] = jnp.where(even, to_left, to_right)

    for g in range(groups):
        at = slice(8 * g, 8 * g + 8)
        block = force_ref[at, :]
        put(
            at,
            jnp.where(here, spin(block, H * f), left_in[at, :]),
            jnp.where(here, spin(block, H * f - (OY - H)), right_in[at, :]),
        )
    at = slice(8 * groups, left_in.shape[0])
    put(at, left_in[at, :], right_in[at, :])


def ocean_kernel(
    sizes, ext_ref, force_ref, first_ref, second_ref, mean_ref, comp_first, comp_second,
    a_ref, wind_ref, src_ref,
    h_out, p_out, send_ref, next_ref, mean2_ref,
):
    AX, AY, LEV, OX, OY, T, SLOT, H, nbh = sizes
    ks = SLOT // 128
    rows = OX + 2 * H
    groups = rows // 8
    lane = iota((8, OY), 1)
    even = parity("tile") == 0
    left_side = chosen(even, second_ref, first_ref)
    right_side = chosen(even, first_ref, second_ref)
    even = parity("comp") == 0
    from_up = chosen(even, comp_second, comp_first)
    from_dn = chosen(even, comp_first, comp_second)
    lefts = [left_side(8 * g, 8 * g + 8) for g in range(groups)]
    rights = [right_side(8 * g, 8 * g + 8) for g in range(groups)]

    def halo(f):
        parts = []
        for g in range(groups):
            from_right = rights[g]
            from_left = lefts[g]
            sr = (-H * f) % OY
            sl = (OY - H - H * f) % OY
            from_right = pltpu.roll(from_right, sr, 1) if sr else from_right
            from_left = pltpu.roll(from_left, sl, 1) if sl else from_left
            parts.append(
                jnp.where(lane < H, from_right, jnp.where(lane >= OY - H, from_left, 0.0))
            )
        return jnp.concatenate(parts, axis=0)

    def wide(f):
        inner = force_ref[...] if f == FIELDS - 1 else ext_ref[f]
        return jnp.concatenate([inner, halo(f)], axis=1)

    height, potential = wide(0), wide(1)
    push = ocean_step * wide(FIELDS - 1)
    moved = {d: wide(2 + o) for o, d in enumerate(ALL_OFFSETS)}
    width = 2 * OY
    for _ in range(SUBCYCLES):
        potential = (1.0 - friction) * potential + (ocean_step * wave_speed) * height + push
        shifted = {
            -1: pltpu.roll(potential, 1, 1),
            0: potential,
            1: pltpu.roll(potential, width - 1, 1),
        }
        part = {
            dr: sum(moved[dr, dc] * shifted[dc] for dc in (-1, 0, 1)) for dr in (-1, 0, 1)
        }
        height = height + part[0] + pltpu.roll(part[1], rows - 1, 0) + pltpu.roll(part[-1], 1, 0)
    final = height[H : H + OX, :OY]
    h_out[...] = final
    p_out[...] = potential[H : H + OX, :OY]

    band = OX * OY // T
    rb = max(1, band // OY)
    source = src_ref[...]
    operands = []
    for r in range(rb):
        operands.append(
            jnp.concatenate(
                [final[(q * band) // OY + r : (q * band) // OY + r + 1, :] for q in range(T)], axis=0
            )
        )
    for k in range(ks):
        index = source[:, 128 * k : 128 * k + 128]
        lanes_at = index & (OY - 1)
        row_at = (index // OY) & (rb - 1)
        value = None
        for r in range(rb):
            got = jnp.take_along_axis(operands[r], lanes_at, axis=1, mode="promise_in_bounds")
            value = got if value is None else jnp.where(row_at == r, got, value)
        for q in range(T):
            send_ref[q, AX + k : AX + k + 1, :] = value[q : q + 1, :]

    base = H * SENT + 2 * nbh * ks + AY * (NP + 1)
    rims_left = left_side(8 * groups, 8 * groups + AX + 2 * NP)
    rims_right = right_side(8 * groups, 8 * groups + AX + 2 * NP)
    state = []
    for i in range(-NP, AX + NP):
        if i < 0:
            before = from_up(base + AY * (i + NP), base + AY * (i + NP + 1))
        elif i >= AX:
            before = from_dn(base + AY * (i - AX), base + AY * (i - AX + 1))
        else:
            before = a_ref[i]
        at = i + NP
        left = rims_left[at : at + 1, :]
        right = rims_right[at : at + 1, :]
        value = before + atmos_step * column_mean(mean_ref[at], left, right)
        state.append(value)
        if 0 <= i < AX:
            next_ref[i] = value
    base = base + AY * NP
    first_c, second_c = column_coefficients(AY, LEV)
    rates = {}
    for i in range(-1, AX + 1):
        start = i - i % NP
        element = [state[start + k + NP] for k in range(NP)]
        if i < 0:
            winds = [from_up(base + AY * m, base + AY * m + AY) for m in range(2)]
        elif i >= AX:
            winds = [from_dn(base + AY * m, base + AY * m + AY) for m in range(2)]
        else:
            winds = [wind_ref[m, i].astype(jnp.float32) for m in range(2)]
        rates[i] = row_rate(element, i % NP, winds[0], winds[1], first_c, second_c)
    for i in range(AX):
        if i % NP == NP - 1:
            value = 0.5 * (rates[i] + rates[i + 1])
        elif i % NP == 0:
            value = 0.5 * (rates[i] + rates[i - 1])
        else:
            value = rates[i]
        mean2_ref[i] = value
    left_edge = mean2_ref[:, 0, :]
    right_edge = mean2_ref[:, AY - 1, :]
    for q in range(T):
        send_ref[q, :AX, :] = jnp.where(
            beside(T, 1) == q, right_edge, jnp.where(beside(T, -1) == q, left_edge, 0.0)
        )


def final_kernel(
    sizes, got_ref, next_ref, mean2_ref, h_ref, p_ref, tgt_ref, wgt_ref,
    a_dst, h_dst, p_dst, flux_dst, a_out, flux_out, sems,
):
    AX, AY, _, _, _, T, SLOT, _, _ = sizes
    copies = [
        pltpu.make_async_copy(source, target, sems.at[k])
        for k, (source, target) in enumerate(
            ((h_ref, h_dst), (p_ref, p_dst), (a_out, a_dst), (flux_out, flux_dst))
        )
    ]
    copies[0].start()
    copies[1].start()
    ks = SLOT // 128
    points = AX * AY // T
    left = got_ref[beside(T, -1), :AX, :]
    right = got_ref[beside(T, 1), :AX, :]
    for i in range(AX):
        a_out[i] = next_ref[i] + atmos_step * column_mean(
            mean2_ref[i], left[i : i + 1], right[i : i + 1]
        )
    copies[2].start()
    base = iota((T, 128), 0) * points
    totals = [jnp.zeros((T, 128), jnp.float32) for _ in range(points)]
    for k in range(ks):
        value = jnp.concatenate([got_ref[q, AX + k : AX + k + 1, :] for q in range(T)], axis=0)
        product = wgt_ref[:, 128 * k : 128 * k + 128] * value
        local = tgt_ref[:, 128 * k : 128 * k + 128] - base
        for m in range(points):
            totals[m] = totals[m] + jnp.where(local == m, product, 0.0)
    for m in range(points):
        flux_out[:, m : m + 1] = jnp.sum(totals[m], axis=1, keepdims=True)
    copies[3].start()
    for copy in copies:
        copy.wait()


def meeting(count, start):
    pairs = []
    for low in range(start, count + start, 2):
        pairs += [(low % count, (low + 1) % count), ((low + 1) % count, low % count)]
    return pairs


def on_device(C, T, *arguments):
    return step(C, T, *arguments)


def step(
    C, T,
    atmos_state, wind_field, ocean_height, ocean_potential, ocean_neighbors, ocean_coupling,
    downward_source, downward_target, downward_weight, upward_source, upward_target, upward_weight,
):
    AX, AY, LEV = atmos_state.shape
    OX, OY = ocean_height.shape
    SLOT = downward_source.shape[-1]
    H = SUBCYCLES
    n = AX * AY
    band = OX * OY // T
    nbh = H * OY // band
    ks = SLOT // 128
    sizes = (AX, AY, LEV, OX, OY, T, SLOT, H, nbh)
    f32, i32 = jnp.float32, jnp.int32
    static_rows = H * SENT + 2 * nbh * ks + AY * (2 * NP + 3)
    front_args = (
        downward_source, atmos_state, wind_field, ocean_neighbors, ocean_coupling,
        ocean_height, ocean_potential, downward_target, downward_weight,
    )
    front_outs = [
        ((C * T, 1, SLOT + 3 * n), f32), ((static_rows, 128), f32), ((static_rows, 128), f32),
        ((FIELDS - 4, OX, OY), f32), ((AX, AY, LEV), f32),
    ]
    slots, comp_first, comp_second, w8, rate = call(
        functools.partial(front_kernel, sizes, C),
        front_outs,
        front_args,
        scratch=[pltpu.VMEM(v.shape, v.dtype) for v in front_args]
        + [pltpu.VMEM(*v) for v in front_outs]
        + [pltpu.SemaphoreType.DMA((14,))],
        raw_in=True,
        raw_out=5,
        limit=None,
    )
    comp_second = lax.ppermute(comp_second, "comp", meeting(C, 1))
    comp_first = lax.ppermute(comp_first, "comp", meeting(C, 0))
    got = lax.all_to_all(slots, ("comp", "tile"), 0, 0, tiled=True)
    got = got.reshape(C * T, SLOT + 3 * n)

    edge_rows = OX + 2 * H + AX + 2 * NP
    NB = T + 2 * nbh
    ext, mean, left, right, high, low, weight = call(
        functools.partial(prepare_kernel, sizes),
        [((FIELDS - 1, OX + 2 * H, OY), f32), ((AX + 2 * NP, AY, LEV), f32)]
        + [((edge_rows, 128), f32)] * 2
        + [((NB, SLOT), i32)] * 2
        + [((NB, SLOT), f32)],
        (
            comp_first, comp_second, ocean_height, ocean_potential, w8,
            downward_target, downward_weight, rate,
        ),
    )
    force, tile_first, tile_second = call(
        functools.partial(remap_kernel, sizes, C),
        [((OX + 2 * H, OY), f32)] + [((edge_rows, 128), f32)] * 2,
        (got, high, low, weight, left, right),
        scratch=[pltpu.VMEM((NB, SLOT), f32)] * 3 + [pltpu.VMEM((NB * band // LOW, OY), f32)],
    )
    tile_second = lax.ppermute(tile_second, "tile", meeting(T, 1))
    tile_first = lax.ppermute(tile_first, "tile", meeting(T, 0))

    height, potential, send, state, mean2 = call(
        functools.partial(ocean_kernel, sizes),
        [((OX, OY), f32)] * 2 + [((T, AX + max(8, ks), 128), f32)] + [((AX, AY, LEV), f32)] * 2,
        (
            ext, force, tile_first, tile_second, mean, comp_first, comp_second,
            atmos_state, wind_field,
            upward_source[0],
        ),
    )
    back = lax.all_to_all(send, "tile", 0, 0, tiled=True)
    atmos, height, potential, flux = call(
        functools.partial(final_kernel, sizes),
        [((AX, AY, LEV), f32)] + [((OX, OY), f32)] * 2 + [((T, n // T), f32)],
        (back, state, mean2, height, potential, upward_target[0], upward_weight[0]),
        scratch=[
            pltpu.VMEM((AX, AY, LEV), f32),
            pltpu.VMEM((T, n // T), f32),
            pltpu.SemaphoreType.DMA((4,)),
        ],
        raw_out=4,
    )
    return (atmos, height, potential, flux.reshape(AX, AY))


def solution(mesh):
    return jax.shard_map(
        functools.partial(on_device, mesh.shape["comp"], mesh.shape["tile"]),
        mesh=mesh,
        in_specs=(
            P("comp", "tile", None),
            P(None, "comp", "tile", None),
            P("comp", "tile"),
            P("comp", "tile"),
            P(None, "comp", "tile"),
            P(None, "comp", "tile"),
            P("comp", "tile", None),
            P("comp", "tile", None),
            P("comp", "tile", None),
            P("comp", "tile", None),
            P("comp", "tile", None),
            P("comp", "tile", None),
        ),
        out_specs=(
            P("comp", "tile", None),
            P("comp", "tile"),
            P("comp", "tile"),
            P("comp", "tile"),
        ),
        check_vma=False,
    )
```

```python
import functools

import jax
import jax.numpy as jnp
import numpy as np
from jax import lax
from jax.experimental import pallas as pl
from jax.experimental.pallas import tpu as pltpu
from jax.sharding import PartitionSpec as P

NP = 4
SUBCYCLES = 8

atmos_step = 0.05
viscosity = 0.05
ocean_step = 0.2
wave_speed = 1.0
friction = 0.05

OFFSETS = [(a, b) for a in (-1, 0, 1) for b in (-1, 0, 1) if (a, b) != (0, 0)]
ALL_OFFSETS = [(a, b) for a in (-1, 0, 1) for b in (-1, 0, 1)]
SENT = 2 + len(OFFSETS)
FIELDS = 3 + len(ALL_OFFSETS)
LOW = 32


def gll_derivative():
    points = np.array([-1.0, -1.0 / np.sqrt(5.0), 1.0 / np.sqrt(5.0), 1.0])
    weights = np.array(
        [1.0 / np.prod([points[j] - points[k] for k in range(4) if k != j]) for j in range(4)]
    )
    matrix = np.zeros((4, 4))
    for i in range(4):
        for j in range(4):
            if i != j:
                matrix[i, j] = weights[j] / weights[i] / (points[i] - points[j])
        matrix[i, i] = -np.sum(matrix[i])
    return matrix


D1 = gll_derivative()
D2 = D1 @ D1


def band_coefficients(position, matrix):
    result = {}
    for shift in range(1 - NP, NP):
        value = jnp.zeros(position.shape, jnp.float32)
        for i in range(NP):
            if 0 <= i + shift < NP:
                value = jnp.where(position == i, float(matrix[i, i + shift]), value)
        result[shift] = value
    return result


def iota(shape, dim):
    return lax.broadcasted_iota(jnp.int32, shape, dim)


def full_specs(count):
    return [pl.BlockSpec(memory_space=pltpu.VMEM) for _ in range(count)]


def call(body, out_shapes, args, scratch=(), raw_in=False, raw_out=0, limit=16):
    raw = pl.BlockSpec(memory_space=pltpu.HBM)
    return pl.pallas_call(
        body,
        out_shape=[jax.ShapeDtypeStruct(s, d) for s, d in out_shapes],
        in_specs=([raw] * len(args) if raw_in else full_specs(len(args))),
        out_specs=[raw] * raw_out + full_specs(len(out_shapes) - raw_out),
        scratch_shapes=list(scratch),
        compiler_params=pltpu.CompilerParams(
            vmem_limit_bytes=limit * 1024 * 1024 if limit else None
        ),
        cost_estimate=pl.CostEstimate(
            flops=1000000, bytes_accessed=1000000, transcendentals=0
        ),
    )(*args)


def column_shift(row, shift):
    extent, levels = row.shape
    tiles = row.reshape(extent // 8, 8, levels)
    return pltpu.roll(tiles, (-shift) % 8, 1).reshape(extent, levels)


def second_terms(row, first_c, second_c):
    slope = first_c[0] * row
    curve = second_c[0] * row
    for shift in range(1 - NP, NP):
        if shift:
            moved = column_shift(row, shift)
            slope = slope + first_c[shift] * moved
            curve = curve + second_c[shift] * moved
    return slope, curve


def row_rate(element, position, wind_east, wind_north, first_c, second_c):
    slope_east = sum(float(D1[position, k]) * element[k] for k in range(NP))
    curve_east = sum(float(D2[position, k]) * element[k] for k in range(NP))
    slope_north, curve_north = second_terms(element[position], first_c, second_c)
    return viscosity * (curve_east + curve_north) - (
        wind_east * slope_east + wind_north * slope_north
    )


def column_mean(row, left_edge, right_edge):
    extent, levels = row.shape
    at = iota((extent, levels), 0)
    after = jnp.where(at == extent - 1, right_edge, pltpu.roll(row, extent - 1, 0))
    before = jnp.where(at == 0, left_edge, pltpu.roll(row, 1, 0))
    position = at % NP
    return jnp.where(
        position == NP - 1,
        0.5 * (row + after),
        jnp.where(position == 0, 0.5 * (row + before), row),
    )


def column_coefficients(extent, levels):
    position = iota((extent, levels), 0) % NP
    return band_coefficients(position, D1), band_coefficients(position, D2)


def front_kernel(sizes, C, *refs):
    AX, AY, LEV, OX, OY, T, SLOT, H, nbh = sizes
    ks = SLOT // 128
    n = AX * AY
    inputs, outputs, held, made, sems = refs[:9], refs[9:14], refs[14:23], refs[23:28], refs[28]
    loads = [pltpu.make_async_copy(inputs[k], held[k], sems.at[k]) for k in range(9)]
    stores = [pltpu.make_async_copy(made[k], outputs[k], sems.at[9 + k]) for k in range(5)]
    for copy in loads:
        copy.start()
    src_ref, a_ref, wind_ref, nbr_ref, cpl_ref, h_ref, p_ref, tgt_ref, wgt_ref = held
    slots_ref, first_ref, second_ref, w8_ref, rate_ref = made
    for copy in loads[:3]:
        copy.wait()
    source = src_ref[0].astype(jnp.float32)
    surface = [
        jnp.transpose(v.astype(jnp.float32).reshape(n, LEV))[LEV - 1 :, :]
        for v in (a_ref[...], wind_ref[0], wind_ref[1])
    ]

    def spread(c, carry):
        for q in range(T):
            at = c * T + q
            slots_ref[at, :, :SLOT] = source[q : q + 1, :]
            for m in range(3):
                slots_ref[at, :, SLOT + n * m : SLOT + n * m + n] = surface[m]
        return carry

    if C <= 4:
        for c in range(C):
            spread(c, 0)
    else:
        lax.fori_loop(0, C, spread, 0)
    stores[0].start()

    even = parity("comp") == 0

    def put(at, to_up, to_dn):
        rows = slice(at, at + to_up.shape[0])
        first_ref[rows, :] = jnp.where(even, to_dn, to_up)
        second_ref[rows, :] = jnp.where(even, to_up, to_dn)

    first_c, second_c = column_coefficients(AY, LEV)
    rates = []
    for i in range(AX):
        start = i - i % NP
        element = [a_ref[start + k] for k in range(NP)]
        rates.append(
            row_rate(
                element,
                i % NP,
                wind_ref[0, i].astype(jnp.float32),
                wind_ref[1, i].astype(jnp.float32),
                first_c,
                second_c,
            )
        )
        rate_ref[i] = rates[i]
    stores[4].start()
    none = jnp.zeros((1, LEV), jnp.float32)
    sides = []
    for rim, step in ((0, 1), (AX - 1, -1)):
        at_rim = rim % NP
        east, north = (wind_ref[m, rim].astype(jnp.float32) for m in range(2))
        others, partial = [], 0.0
        for d in range(1, NP):
            i = rim + step * d
            mean = 0.5 * (rates[i] + rates[i + step]) if d == NP - 1 else rates[i]
            others.append(mean)
            state = a_ref[i] + atmos_step * column_mean(mean, none, none)
            at_i = i % NP
            partial = partial + (
                viscosity * float(D2[at_rim, at_i]) - east * float(D1[at_rim, at_i])
            ) * state
        edges = jnp.concatenate(
            [v[:1] for v in others] + [v[AY - 1 :] for v in others] + [none] * 2, axis=0
        )
        own = a_ref[rim]
        slope, curve = second_terms(own, first_c, second_c)
        partial = (
            partial
            + viscosity * (float(D2[at_rim, at_rim]) * own + curve)
            - (east * (float(D1[at_rim, at_rim]) * own) + north * slope)
        )
        sides.append([rates[rim], partial, east, north, edges])
    at = H * SENT + 2 * nbh * ks
    for to_up, to_dn in zip(*sides):
        put(at, to_up, to_dn)
        at += to_up.shape[0]

    for copy in loads[3:]:
        copy.wait()
    centre = (iota((OX, OY), 0) + 1) * (OY + 2) + iota((OX, OY), 1) + 1
    offset = [nbr_ref[l] - centre for l in range(6)]
    coupling = [cpl_ref[l] for l in range(6)]
    fields = [h_ref[...], p_ref[...]]
    for o, (dr, dc) in enumerate(OFFSETS):
        code = dr * (OY + 2) + dc
        layer = jnp.zeros((OX, OY), jnp.float32)
        for l in range(6):
            layer = layer + jnp.where(offset[l] == code, coupling[l], 0.0)
        w8_ref[o] = layer
        fields.append(layer)
    stores[3].start()
    for f, field in enumerate(fields):
        put(H * f, field[:H], field[OX - H :])
    at = H * SENT
    for ref in (tgt_ref, wgt_ref):
        table = ref[0].astype(jnp.float32)
        for k in range(ks):
            chunk = table[:, 128 * k : 128 * k + 128]
            put(at, chunk[:nbh], chunk[T - nbh :])
            at += nbh
    stores[1].start()
    stores[2].start()
    for copy in stores:
        copy.wait()


def parity(axis):
    return lax.rem(lax.axis_index(axis), 2)


def beside(count, step):
    return lax.rem(lax.axis_index("tile") + step + count, count)


def chosen(flag, one, other):
    return lambda lo, hi: jnp.where(flag, one[lo:hi, :], other[lo:hi, :])


def surface_coefficients(shape, stride, matrix):
    return band_coefficients((iota(shape, 1) // stride) % NP, matrix)


def surface_steps(blocks, winds, AX, AY):
    shape = blocks[0].shape
    n = AX * AY
    lane = iota(shape, 1)
    i_at, j_at = lane // AY, lane % AY
    x1 = surface_coefficients(shape, AY, D1)
    x2 = surface_coefficients(shape, AY, D2)
    y1 = surface_coefficients(shape, 1, D1)
    y2 = surface_coefficients(shape, 1, D2)

    def lanes(v, shift):
        return pltpu.roll(v, (-shift) % n, 1) if shift % n else v

    def rate(v, east, north):
        slope_e, slope_n, curve = x1[0] * v, y1[0] * v, (x2[0] + y2[0]) * v
        for s in range(1 - NP, NP):
            if s:
                along = lanes(v, s * AY)
                slope_e = slope_e + x1[s] * along
                curve = curve + x2[s] * along
                along = lanes(v, s)
                slope_n = slope_n + y1[s] * along
                curve = curve + y2[s] * along
        return viscosity * curve - (east * slope_e + north * slope_n)

    def mean_columns(v):
        devices = shape[0]
        following = pltpu.roll(v, devices - 1, 0)
        preceding = pltpu.roll(v, 1, 0)
        after = jnp.where(j_at == AY - 1, lanes(following, 1 - AY), lanes(v, 1))
        before = jnp.where(j_at == 0, lanes(preceding, AY - 1), lanes(v, -1))
        return jnp.where(
            j_at % NP == NP - 1,
            0.5 * (v + after),
            jnp.where(j_at % NP == 0, 0.5 * (v + before), v),
        )

    def mean_rows(v, above, below):
        after = jnp.where(i_at == AX - 1, lanes(below, AY - n), lanes(v, AY))
        before = jnp.where(i_at == 0, lanes(above, n - AY), lanes(v, -AY))
        return jnp.where(
            i_at % NP == NP - 1,
            0.5 * (v + after),
            jnp.where(i_at % NP == 0, 0.5 * (v + before), v),
        )

    for _ in range(2):
        across = [mean_columns(rate(v, e, w)) for v, (e, w) in zip(blocks, winds)]
        count = len(blocks)
        blocks = [
            blocks[b]
            + atmos_step
            * mean_rows(across[b], across[max(b - 1, 0)], across[min(b + 1, count - 1)])
            for b in range(count)
        ]
    return blocks


def prepare_kernel(
    sizes, first_ref, second_ref, h_ref, p_ref, w8_ref, tgt_ref, wgt_ref, rate_ref,
    ext_ref, mean_ref, left_ref, right_ref, high_ref, low_ref, weight_ref,
):
    AX, AY, _, OX, OY, T, SLOT, H, nbh = sizes
    ks = SLOT // 128
    band = OX * OY // T
    static_fields = FIELDS - 1

    even = parity("comp") == 0
    from_up = chosen(even, second_ref, first_ref)
    from_dn = chosen(even, first_ref, second_ref)

    base = H * SENT + 2 * nbh * ks
    rates = [from_up(base, base + AY)] + [rate_ref[i] for i in range(AX)]
    rates.append(from_dn(base, base + AY))
    for i in range(-1, AX + 1):
        at = i + 1
        if i == -1 or i < AX and i % NP == NP - 1:
            value = 0.5 * (rates[at] + rates[at + 1])
        elif i % NP == 0:
            value = 0.5 * (rates[at] + rates[at - 1])
        else:
            value = rates[at]
        mean_ref[at] = value
    groups = (OX + 2 * H) // 8
    base = base + 4 * AY
    m = NP - 1
    up_edges, dn_edges = from_up(base, base + 8), from_dn(base, base + 8)
    for ref, j, lo in ((left_ref, 0, 0), (right_ref, AY - 1, m)):
        at = 8 * groups
        ref[at : at + AX + 2, :] = mean_ref[:, j, :]
        ref[at + AX + 2 : at + AX + 2 + m, :] = up_edges[lo : lo + m]
        ref[at + AX + 2 + m : at + AX + 2 + 2 * m, :] = dn_edges[lo : lo + m]

    base = H * SENT
    for k in range(ks):
        at = slice(128 * k, 128 * k + 128)
        t_lo, w_lo = base + k * nbh, base + (ks + k) * nbh
        for lo, count, target, weight in (
            (0, nbh, from_up(t_lo, t_lo + nbh), from_up(w_lo, w_lo + nbh)),
            (nbh, T, tgt_ref[0, :, at], wgt_ref[0, :, at]),
            (nbh + T, nbh, from_dn(t_lo, t_lo + nbh), from_dn(w_lo, w_lo + nbh)),
        ):
            target = target.astype(jnp.int32)
            weight_ref[lo : lo + count, at] = weight
            high_ref[lo : lo + count, at] = (target & (band - 1)) // LOW
            low_ref[lo : lo + count, at] = target & (LOW - 1)

    rows = OX + 2 * H

    def extended(f):
        own = h_ref[...] if f == 0 else p_ref[...] if f == 1 else w8_ref[f - 2]
        return jnp.concatenate(
            [from_up(H * f, H * f + H), own, from_dn(H * f, H * f + H)], axis=0
        )

    ext_ref[0] = extended(0)
    ext_ref[1] = extended(1)
    layers = {d: ocean_step * extended(2 + o) for o, d in enumerate(OFFSETS)}
    layers[0, 0] = -sum(layers[d] for d in OFFSETS)
    for o, d in enumerate(ALL_OFFSETS):
        ext_ref[2 + o] = pltpu.roll(layers[d], d[0] % rows, 0) if d[0] else layers[d]
    for g in range(groups):
        low = jnp.zeros((8, OY), jnp.float32)
        high = jnp.zeros((8, OY), jnp.float32)
        for f in range(static_fields):
            low, high = pack(low, high, ext_ref[f, 8 * g : 8 * g + 8, :], f, H)
        left_ref[8 * g : 8 * g + 8, :] = low
        right_ref[8 * g : 8 * g + 8, :] = high


def pack(low, high, block, f, H):
    count = block.shape[1] // H
    at = iota(block.shape, 1) // H
    low = jnp.where(at == (f + count // 2) % count, spin(block, H * (f + count // 2)), low)
    high = jnp.where(at == (f - 1) % count, spin(block, H * f), high)
    return low, high


def spin(value, shift):
    shift = shift % value.shape[1]
    return pltpu.roll(value, shift, 1) if shift else value


def remap_kernel(
    sizes, C, got_ref, high_ref, low_ref, weight_ref, left_in, right_in,
    force_ref, first_ref, second_ref, hi_s, mid_s, lo_s, placed_s,
):
    AX, AY, _, OX, OY, T, SLOT, H, nbh = sizes
    ks = SLOT // 128
    n = AX * AY
    NB = T + 2 * nbh
    band = OX * OY // T
    groups = (OX + 2 * H) // 8

    def row_of(k):
        return lax.rem(lax.axis_index("comp") + (k - 2) + C, C)

    def slot(c, lo, hi):
        return got_ref[pl.ds(pl.multiple_of(row_of(c) * T, T), T), lo:hi]

    blocks = [slot(k, SLOT, SLOT + n) for k in range(5)]
    winds = [
        (slot(k, SLOT + n, SLOT + 2 * n), slot(k, SLOT + 2 * n, SLOT + 3 * n))
        for k in range(5)
    ]
    final = surface_steps(blocks, winds, AX, AY)[1:4]

    for k in range(ks):
        at = slice(128 * k, 128 * k + 128)
        picked = [
            jnp.take_along_axis(
                final[b], slot(1 + b, 128 * k, 128 * k + 128).astype(jnp.int32), axis=1,
                mode="promise_in_bounds",
            )
            for b in range(3)
        ]
        for lo, count, value in (
            (0, nbh, picked[0][T - nbh :]),
            (nbh, T, picked[1]),
            (nbh + T, nbh, picked[2][:nbh]),
        ):
            product = weight_ref[lo : lo + count, at] * value
            hi = product.astype(jnp.bfloat16).astype(jnp.float32)
            rest = product - hi
            mid = rest.astype(jnp.bfloat16).astype(jnp.float32)
            hi_s[lo : lo + count, at] = hi
            mid_s[lo : lo + count, at] = mid
            lo_s[lo : lo + count, at] = rest - mid

    count = band // LOW
    high_at = iota((count, SLOT), 0)
    low_at = iota((LOW, SLOT), 0)
    for b in range(NB):
        row = slice(b, b + 1)
        chosen = high_ref[row, :] == high_at
        left = jnp.concatenate(
            [jnp.where(chosen, ref[row, :], 0.0) for ref in (hi_s, mid_s, lo_s)], axis=0
        ).astype(jnp.bfloat16)
        hot = jnp.where(low_ref[row, :] == low_at, 1.0, 0.0).astype(jnp.bfloat16)
        placed = lax.dot_general(
            left, hot, (((1,), (1,)), ((), ())), preferred_element_type=jnp.float32
        )
        placed_s[count * b : count * b + count, :LOW] = (
            placed[:count] + placed[count : 2 * count] + placed[2 * count :]
        )
    pieces = OY // LOW
    lane_piece = iota((OX + 2 * H, OY), 1) // LOW
    force = None
    for q in range(pieces):
        piece = spin(placed_s[pl.ds(q, OX + 2 * H, stride=pieces), :], LOW * q)
        force = piece if force is None else jnp.where(lane_piece == q, piece, force)
    force_ref[...] = force

    f = FIELDS - 1
    even = parity("tile") == 0

    def put(rows, to_left, to_right):
        first_ref[rows, :] = jnp.where(even, to_right, to_left)
        second_ref[rows, :] = jnp.where(even, to_left, to_right)

    for g in range(groups):
        at = slice(8 * g, 8 * g + 8)
        put(at, *pack(left_in[at, :], right_in[at, :], force_ref[at, :], f, H))
    at = slice(8 * groups, left_in.shape[0])
    put(at, left_in[at, :], right_in[at, :])


def subcycles(height, potential, push, layers):
    rows, width = height.shape
    for _ in range(SUBCYCLES):
        potential = (1.0 - friction) * potential + (ocean_step * wave_speed) * height + push
        shifted = {
            -1: pltpu.roll(potential, 1, 1),
            0: potential,
            1: pltpu.roll(potential, width - 1, 1),
        }
        part = {
            dr: sum(layers[dr, dc] * shifted[dc] for dc in (-1, 0, 1)) for dr in (-1, 0, 1)
        }
        height = height + part[0] + pltpu.roll(part[1], rows - 1, 0) + pltpu.roll(part[-1], 1, 0)
    return height, potential


def inner_kernel(sizes, ext_ref, force_ref, h_ref, p_ref, strip_ref):
    _, _, _, OX, OY, _, _, H, _ = sizes
    fields = [ext_ref[f] for f in range(FIELDS - 1)] + [force_ref[...]]
    lane = iota(fields[0].shape, 1)
    for f, field in enumerate(fields):
        strip_ref[f] = jnp.where(
            lane < 2 * H,
            field,
            jnp.where((lane >= OY // 2 - 2 * H) & (lane < OY // 2), spin(field, OY // 2), 0.0),
        )
    height, potential = subcycles(
        fields[0], fields[1], ocean_step * fields[-1],
        {d: fields[2 + o] for o, d in enumerate(ALL_OFFSETS)},
    )
    h_ref[...] = height[H : H + OX]
    p_ref[...] = potential[H : H + OX]


def ocean_kernel(
    sizes, strip_ref, h_ref, p_ref, first_ref, second_ref, mean_ref, comp_first, comp_second,
    a_ref, wind_ref, src_ref,
    h_out, p_out, send_ref, next_ref, mean2_ref,
):
    AX, AY, LEV, OX, OY, T, SLOT, H, nbh = sizes
    ks = SLOT // 128
    rows = OX + 2 * H
    groups = rows // 8
    lane = iota((8, OY), 1)
    even = parity("tile") == 0
    left_side = chosen(even, second_ref, first_ref)
    right_side = chosen(even, first_ref, second_ref)
    even = parity("comp") == 0
    from_up = chosen(even, comp_second, comp_first)
    from_dn = chosen(even, comp_first, comp_second)

    odd_slot = (lane // H) % 2 == 1
    mixed = []
    for g in range(groups):
        left, right = left_side(8 * g, 8 * g + 8), right_side(8 * g, 8 * g + 8)
        mixed.append((jnp.where(odd_slot, left, right), jnp.where(odd_slot, right, left)))
    halo = (lane >= OY - H) | (lane >= OY // 2) & (lane < OY // 2 + H)
    fields = [
        jnp.concatenate(
            [
                jnp.where(
                    halo, spin(mixed[g][f % 2], -H * f), strip_ref[f, 8 * g : 8 * g + 8, :]
                )
                for g in range(groups)
            ],
            axis=0,
        )
        for f in range(FIELDS)
    ]
    edge_h, edge_p = subcycles(
        fields[0], fields[1], ocean_step * fields[-1],
        {d: fields[2 + o] for o, d in enumerate(ALL_OFFSETS)},
    )
    lane = iota((OX, OY), 1)

    def merge(inner, edge):
        edge = edge[H : H + OX]
        return jnp.where(
            lane < H, edge, jnp.where(lane >= OY - H, spin(edge, OY // 2), inner)
        )

    final = merge(h_ref[...], edge_h)
    h_out[...] = final
    p_out[...] = merge(p_ref[...], edge_p)

    band = OX * OY // T
    rb = max(1, band // OY)
    source = src_ref[...]
    operands = []
    for r in range(rb):
        operands.append(
            jnp.concatenate(
                [final[(q * band) // OY + r : (q * band) // OY + r + 1, :] for q in range(T)], axis=0
            )
        )
    for k in range(ks):
        index = source[:, 128 * k : 128 * k + 128]
        lanes_at = index & (OY - 1)
        row_at = (index // OY) & (rb - 1)
        value = None
        for r in range(rb):
            got = jnp.take_along_axis(operands[r], lanes_at, axis=1, mode="promise_in_bounds")
            value = got if value is None else jnp.where(row_at == r, got, value)
        for q in range(T):
            send_ref[q, AX + k : AX + k + 1, :] = value[q : q + 1, :]

    base = H * SENT + 2 * nbh * ks
    at = 8 * groups
    rims_left = left_side(at, at + AX + 2 * NP)
    rims_right = right_side(at, at + AX + 2 * NP)
    first_c, second_c = column_coefficients(AY, LEV)
    column_at = iota((AY, LEV), 0)

    def advance(i, before):
        at = i + 1
        return before + atmos_step * column_mean(
            mean_ref[at], rims_left[at : at + 1, :], rims_right[at : at + 1, :]
        )

    state = [advance(i, a_ref[i]) for i in range(AX)]
    rates = {}
    for i in range(AX):
        next_ref[i] = state[i]
        start = i - i % NP
        winds = [wind_ref[m, i].astype(jnp.float32) for m in range(2)]
        rates[i] = row_rate(state[start : start + NP], i % NP, *winds, first_c, second_c)
    for i, side, at_rim, step, lo in (
        (-1, from_up, NP - 1, -1, AX + 2), (AX, from_dn, 0, 1, AX + 1 + NP)
    ):
        partial, east, north = (
            side(base + AY * k, base + AY * k + AY) for k in range(1, 4)
        )
        rim = advance(i, 0.0)
        slope_north, curve_north = second_terms(rim, first_c, second_c)
        slope_east = float(D1[at_rim, at_rim]) * rim
        curve_east = float(D2[at_rim, at_rim]) * rim
        for d in range(1, NP):
            at = lo + d - 1
            edge = (0.5 * atmos_step) * jnp.where(
                column_at == 0,
                rims_left[at : at + 1, :],
                jnp.where(column_at == AY - 1, rims_right[at : at + 1, :], 0.0),
            )
            slope_east = slope_east + float(D1[at_rim, at_rim + step * d]) * edge
            curve_east = curve_east + float(D2[at_rim, at_rim + step * d]) * edge
        rates[i] = (
            partial
            + viscosity * (curve_east + curve_north)
            - (east * slope_east + north * slope_north)
        )
    for i in range(AX):
        if i % NP == NP - 1:
            value = 0.5 * (rates[i] + rates[i + 1])
        elif i % NP == 0:
            value = 0.5 * (rates[i] + rates[i - 1])
        else:
            value = rates[i]
        mean2_ref[i] = value
    left_edge = mean2_ref[:, 0, :]
    right_edge = mean2_ref[:, AY - 1, :]
    for q in range(T):
        send_ref[q, :AX, :] = jnp.where(
            beside(T, 1) == q, right_edge, jnp.where(beside(T, -1) == q, left_edge, 0.0)
        )


def final_kernel(
    sizes, got_ref, next_ref, mean2_ref, h_ref, p_ref, tgt_ref, wgt_ref,
    a_dst, h_dst, p_dst, flux_dst, a_out, flux_out, sems,
):
    AX, AY, _, _, _, T, SLOT, _, _ = sizes
    copies = [
        pltpu.make_async_copy(source, target, sems.at[k])
        for k, (source, target) in enumerate(
            ((h_ref, h_dst), (p_ref, p_dst), (a_out, a_dst), (flux_out, flux_dst))
        )
    ]
    copies[0].start()
    copies[1].start()
    ks = SLOT // 128
    points = AX * AY // T
    left = got_ref[beside(T, -1), :AX, :]
    right = got_ref[beside(T, 1), :AX, :]
    for i in range(AX):
        a_out[i] = next_ref[i] + atmos_step * column_mean(
            mean2_ref[i], left[i : i + 1], right[i : i + 1]
        )
    copies[2].start()
    base = iota((T, 128), 0) * points
    totals = [jnp.zeros((T, 128), jnp.float32) for _ in range(points)]
    for k in range(ks):
        value = jnp.concatenate([got_ref[q, AX + k : AX + k + 1, :] for q in range(T)], axis=0)
        product = wgt_ref[:, 128 * k : 128 * k + 128] * value
        local = tgt_ref[:, 128 * k : 128 * k + 128] - base
        for m in range(points):
            totals[m] = totals[m] + jnp.where(local == m, product, 0.0)
    for m in range(points):
        flux_out[:, m : m + 1] = jnp.sum(totals[m], axis=1, keepdims=True)
    copies[3].start()
    for copy in copies:
        copy.wait()


def meeting(count, start):
    pairs = []
    for low in range(start, count + start, 2):
        pairs += [(low % count, (low + 1) % count), ((low + 1) % count, low % count)]
    return pairs


def on_device(C, T, *arguments):
    return step(C, T, *arguments)


def step(
    C, T,
    atmos_state, wind_field, ocean_height, ocean_potential, ocean_neighbors, ocean_coupling,
    downward_source, downward_target, downward_weight, upward_source, upward_target, upward_weight,
):
    AX, AY, LEV = atmos_state.shape
    OX, OY = ocean_height.shape
    SLOT = downward_source.shape[-1]
    H = SUBCYCLES
    n = AX * AY
    band = OX * OY // T
    nbh = H * OY // band
    ks = SLOT // 128
    sizes = (AX, AY, LEV, OX, OY, T, SLOT, H, nbh)
    f32, i32 = jnp.float32, jnp.int32
    static_rows = H * SENT + 2 * nbh * ks + 4 * AY + 8
    front_args = (
        downward_source, atmos_state, wind_field, ocean_neighbors, ocean_coupling,
        ocean_height, ocean_potential, downward_target, downward_weight,
    )
    front_outs = [
        ((C * T, 1, SLOT + 3 * n), f32), ((static_rows, 128), f32), ((static_rows, 128), f32),
        ((FIELDS - 4, OX, OY), f32), ((AX, AY, LEV), f32),
    ]
    slots, comp_first, comp_second, w8, rate = call(
        functools.partial(front_kernel, sizes, C),
        front_outs,
        front_args,
        scratch=[pltpu.VMEM(v.shape, v.dtype) for v in front_args]
        + [pltpu.VMEM(*v) for v in front_outs]
        + [pltpu.SemaphoreType.DMA((14,))],
        raw_in=True,
        raw_out=5,
        limit=None,
    )
    comp_second = lax.ppermute(comp_second, "comp", meeting(C, 1))
    comp_first = lax.ppermute(comp_first, "comp", meeting(C, 0))
    got = lax.all_to_all(slots, ("comp", "tile"), 0, 0, tiled=True)
    got = got.reshape(C * T, SLOT + 3 * n)

    edge_rows = OX + 2 * H + AX + 2 * NP
    NB = T + 2 * nbh
    ext, mean, left, right, high, low, weight = call(
        functools.partial(prepare_kernel, sizes),
        [((FIELDS - 1, OX + 2 * H, OY), f32), ((AX + 2, AY, LEV), f32)]
        + [((edge_rows, 128), f32)] * 2
        + [((NB, SLOT), i32)] * 2
        + [((NB, SLOT), f32)],
        (
            comp_first, comp_second, ocean_height, ocean_potential, w8,
            downward_target, downward_weight, rate,
        ),
    )
    force, tile_first, tile_second = call(
        functools.partial(remap_kernel, sizes, C),
        [((OX + 2 * H, OY), f32)] + [((edge_rows, 128), f32)] * 2,
        (got, high, low, weight, left, right),
        scratch=[pltpu.VMEM((NB, SLOT), f32)] * 3 + [pltpu.VMEM((NB * band // LOW, OY), f32)],
    )
    tile_second = lax.ppermute(tile_second, "tile", meeting(T, 1))
    tile_first = lax.ppermute(tile_first, "tile", meeting(T, 0))

    inner_h, inner_p, strips = call(
        functools.partial(inner_kernel, sizes),
        [((OX, OY), f32)] * 2 + [((FIELDS, OX + 2 * H, OY), f32)],
        (ext, force),
    )
    height, potential, send, state, mean2 = call(
        functools.partial(ocean_kernel, sizes),
        [((OX, OY), f32)] * 2 + [((T, AX + max(8, ks), 128), f32)] + [((AX, AY, LEV), f32)] * 2,
        (
            strips, inner_h, inner_p, tile_first, tile_second, mean, comp_first, comp_second,
            atmos_state, wind_field, upward_source[0],
        ),
    )
    back = lax.all_to_all(send, "tile", 0, 0, tiled=True)
    atmos, height, potential, flux = call(
        functools.partial(final_kernel, sizes),
        [((AX, AY, LEV), f32)] + [((OX, OY), f32)] * 2 + [((T, n // T), f32)],
        (back, state, mean2, height, potential, upward_target[0], upward_weight[0]),
        scratch=[
            pltpu.VMEM((AX, AY, LEV), f32),
            pltpu.VMEM((T, n // T), f32),
            pltpu.SemaphoreType.DMA((4,)),
        ],
        raw_out=4,
    )
    return (atmos, height, potential, flux.reshape(AX, AY))


def solution(mesh):
    return jax.shard_map(
        functools.partial(on_device, mesh.shape["comp"], mesh.shape["tile"]),
        mesh=mesh,
        in_specs=(
            P("comp", "tile", None),
            P(None, "comp", "tile", None),
            P("comp", "tile"),
            P("comp", "tile"),
            P(None, "comp", "tile"),
            P(None, "comp", "tile"),
            P("comp", "tile", None),
            P("comp", "tile", None),
            P("comp", "tile", None),
            P("comp", "tile", None),
            P("comp", "tile", None),
            P("comp", "tile", None),
        ),
        out_specs=(
            P("comp", "tile", None),
            P("comp", "tile"),
            P("comp", "tile"),
            P("comp", "tile"),
        ),
        check_vma=False,
    )
```

```python
import functools

import jax
import jax.numpy as jnp
import numpy as np
from jax import lax
from jax.experimental import pallas as pl
from jax.experimental.pallas import tpu as pltpu
from jax.sharding import PartitionSpec as P

NP = 4
SUBCYCLES = 8

atmos_step = 0.05
viscosity = 0.05
ocean_step = 0.2
wave_speed = 1.0
friction = 0.05

OFFSETS = [(a, b) for a in (-1, 0, 1) for b in (-1, 0, 1) if (a, b) != (0, 0)]
ALL_OFFSETS = [(a, b) for a in (-1, 0, 1) for b in (-1, 0, 1)]
SENT = 2 + len(OFFSETS)
FIELDS = 3 + len(ALL_OFFSETS)
LOW = 32
SHIFTS = [s for s in range(1 - NP, NP) if s]


def gll_derivative():
    points = np.array([-1.0, -1.0 / np.sqrt(5.0), 1.0 / np.sqrt(5.0), 1.0])
    weights = np.array(
        [1.0 / np.prod([points[j] - points[k] for k in range(4) if k != j]) for j in range(4)]
    )
    matrix = np.zeros((4, 4))
    for i in range(4):
        for j in range(4):
            if i != j:
                matrix[i, j] = weights[j] / weights[i] / (points[i] - points[j])
        matrix[i, i] = -np.sum(matrix[i])
    return matrix


D1 = gll_derivative()
D2 = D1 @ D1


def band_coefficients(position, matrix):
    result = {}
    for shift in range(1 - NP, NP):
        value = jnp.zeros(position.shape, jnp.float32)
        for i in range(NP):
            if 0 <= i + shift < NP:
                value = jnp.where(position == i, float(matrix[i, i + shift]), value)
        result[shift] = value
    return result


def sum_pairs(terms):
    while len(terms) > 1:
        terms = [sum(terms[k : k + 2][1:], terms[k]) for k in range(0, len(terms), 2)]
    return terms[0]


def iota(shape, dim):
    return lax.broadcasted_iota(jnp.int32, shape, dim)


def full_specs(count):
    return [pl.BlockSpec(memory_space=pltpu.VMEM) for _ in range(count)]


def call(body, out_shapes, args, scratch=(), raw_in=False, raw_out=0, limit=16):
    raw = pl.BlockSpec(memory_space=pltpu.HBM)
    return pl.pallas_call(
        body,
        out_shape=[jax.ShapeDtypeStruct(s, d) for s, d in out_shapes],
        in_specs=([raw] * len(args) if raw_in else full_specs(len(args))),
        out_specs=[raw] * raw_out + full_specs(len(out_shapes) - raw_out),
        scratch_shapes=list(scratch),
        compiler_params=pltpu.CompilerParams(
            vmem_limit_bytes=limit * 1024 * 1024 if limit else None
        ),
        cost_estimate=pl.CostEstimate(
            flops=1000000, bytes_accessed=1000000, transcendentals=0
        ),
    )(*args)


def column_shift(row, shift):
    extent, levels = row.shape
    tiles = row.reshape(extent // 8, 8, levels)
    return pltpu.roll(tiles, (-shift) % 8, 1).reshape(extent, levels)


def second_terms(row, first_c, second_c):
    slope = first_c[0] * row
    curve = second_c[0] * row
    for shift in range(1 - NP, NP):
        if shift:
            moved = column_shift(row, shift)
            slope = slope + first_c[shift] * moved
            curve = curve + second_c[shift] * moved
    return slope, curve


def row_rate(element, position, wind_east, wind_north, first_c, second_c):
    slope_east = sum(float(D1[position, k]) * element[k] for k in range(NP))
    curve_east = sum(float(D2[position, k]) * element[k] for k in range(NP))
    slope_north, curve_north = second_terms(element[position], first_c, second_c)
    return viscosity * (curve_east + curve_north) - (
        wind_east * slope_east + wind_north * slope_north
    )


def column_mean(row, left_edge, right_edge):
    extent, levels = row.shape
    at = iota((extent, levels), 0)
    after = jnp.where(at == extent - 1, right_edge, pltpu.roll(row, extent - 1, 0))
    before = jnp.where(at == 0, left_edge, pltpu.roll(row, 1, 0))
    position = at % NP
    other = jnp.where(position == NP - 1, after, jnp.where(position == 0, before, row))
    return 0.5 * (row + other)


def column_coefficients(extent, levels):
    position = iota((extent, levels), 0) % NP
    return band_coefficients(position, D1), band_coefficients(position, D2)


def front_kernel(sizes, C, *refs):
    AX, AY, LEV, OX, OY, T, SLOT, H, nbh = sizes
    ks = SLOT // 128
    n = AX * AY
    inputs, outputs, held, made, sems = refs[:9], refs[9:14], refs[14:23], refs[23:28], refs[28]
    loads = [pltpu.make_async_copy(inputs[k], held[k], sems.at[k]) for k in range(9)]
    stores = [pltpu.make_async_copy(made[k], outputs[k], sems.at[9 + k]) for k in range(5)]
    for copy in loads:
        copy.start()
    src_ref, a_ref, wind_ref, nbr_ref, cpl_ref, h_ref, p_ref, tgt_ref, wgt_ref = held
    slots_ref, first_ref, second_ref, w8_ref, rate_ref = made
    for copy in loads[:3]:
        copy.wait()
    source = src_ref[0].astype(jnp.float32)
    surface = [
        jnp.transpose(v.astype(jnp.float32).reshape(n, LEV))[LEV - 1 :, :]
        for v in (a_ref[...], wind_ref[0], wind_ref[1])
    ]

    def spread(c, carry):
        for q in range(T):
            at = c * T + q
            slots_ref[at, :, :SLOT] = source[q : q + 1, :]
            for m in range(3):
                slots_ref[at, :, SLOT + n * m : SLOT + n * m + n] = surface[m]
        return carry

    if C <= 4:
        for c in range(C):
            spread(c, 0)
    else:
        lax.fori_loop(0, C, spread, 0)
    stores[0].start()

    even = parity("comp") == 0

    def put(at, to_up, to_dn):
        rows = slice(at, at + to_up.shape[0])
        first_ref[rows, :] = jnp.where(even, to_dn, to_up)
        second_ref[rows, :] = jnp.where(even, to_up, to_dn)

    first_c, second_c = column_coefficients(AY, LEV)
    rates = []
    for i in range(AX):
        start = i - i % NP
        element = [a_ref[start + k] for k in range(NP)]
        rates.append(
            row_rate(
                element,
                i % NP,
                wind_ref[0, i].astype(jnp.float32),
                wind_ref[1, i].astype(jnp.float32),
                first_c,
                second_c,
            )
        )
        rate_ref[i] = rates[i]
    stores[4].start()
    none = jnp.zeros((1, LEV), jnp.float32)
    sides = []
    for rim, step in ((0, 1), (AX - 1, -1)):
        at_rim = rim % NP
        east, north = (wind_ref[m, rim].astype(jnp.float32) for m in range(2))
        others, partial = [], 0.0
        for d in range(1, NP):
            i = rim + step * d
            mean = 0.5 * (rates[i] + rates[i + step]) if d == NP - 1 else rates[i]
            others.append(mean)
            state = a_ref[i] + atmos_step * column_mean(mean, none, none)
            at_i = i % NP
            partial = partial + (
                viscosity * float(D2[at_rim, at_i]) - east * float(D1[at_rim, at_i])
            ) * state
        edges = jnp.concatenate(
            [v[:1] for v in others] + [v[AY - 1 :] for v in others] + [none] * 2, axis=0
        )
        own = a_ref[rim]
        slope, curve = second_terms(own, first_c, second_c)
        partial = (
            partial
            + viscosity * (float(D2[at_rim, at_rim]) * own + curve)
            - (east * (float(D1[at_rim, at_rim]) * own) + north * slope)
        )
        sides.append([rates[rim], partial, east, north, edges])
    at = H * SENT + 2 * nbh * ks
    for to_up, to_dn in zip(*sides):
        put(at, to_up, to_dn)
        at += to_up.shape[0]

    for copy in loads[3:]:
        copy.wait()
    centre = (iota((OX, OY), 0) + 1) * (OY + 2) + iota((OX, OY), 1) + 1
    offset = [nbr_ref[l] - centre for l in range(6)]
    coupling = [cpl_ref[l] for l in range(6)]
    fields = [h_ref[...], p_ref[...]]
    for o, (dr, dc) in enumerate(OFFSETS):
        code = dr * (OY + 2) + dc
        layer = jnp.zeros((OX, OY), jnp.float32)
        for l in range(6):
            layer = layer + jnp.where(offset[l] == code, coupling[l], 0.0)
        w8_ref[o] = layer
        fields.append(layer)
    stores[3].start()
    for f, field in enumerate(fields):
        put(H * f, field[:H], field[OX - H :])
    at = H * SENT
    for ref in (tgt_ref, wgt_ref):
        table = ref[0].astype(jnp.float32)
        for k in range(ks):
            chunk = table[:, 128 * k : 128 * k + 128]
            put(at, chunk[:nbh], chunk[T - nbh :])
            at += nbh
    stores[1].start()
    stores[2].start()
    for copy in stores:
        copy.wait()


def parity(axis):
    return lax.rem(lax.axis_index(axis), 2)


def beside(count, step):
    return lax.rem(lax.axis_index("tile") + step + count, count)


def chosen(flag, one, other):
    return lambda lo, hi: jnp.where(flag, one[lo:hi, :], other[lo:hi, :])


def surface_coefficients(shape, stride, matrix):
    return band_coefficients((iota(shape, 1) // stride) % NP, matrix)


def surface_steps(blocks, winds, AX, AY):
    shape = blocks[0].shape
    n = AX * AY
    lane = iota(shape, 1)
    i_at, j_at = lane // AY, lane % AY
    x1 = surface_coefficients(shape, AY, D1)
    x2 = surface_coefficients(shape, AY, D2)
    y1 = surface_coefficients(shape, 1, D1)
    y2 = surface_coefficients(shape, 1, D2)

    def lanes(v, shift):
        return pltpu.roll(v, (-shift) % n, 1) if shift % n else v

    coefficients = []
    for east, north in winds:
        own = {(0, 0): viscosity * (x2[0] + y2[0]) - (east * x1[0] + north * y1[0])}
        for s in SHIFTS:
            own[s, 0] = viscosity * x2[s] - east * x1[s]
            own[0, s] = viscosity * y2[s] - north * y1[s]
        coefficients.append(own)

    def rate(v, own):
        return sum_pairs([field * lanes(v, s * AY + r) for (s, r), field in own.items()])

    def mean_columns(v):
        devices = shape[0]
        following = pltpu.roll(v, devices - 1, 0)
        preceding = pltpu.roll(v, 1, 0)
        after = jnp.where(j_at == AY - 1, lanes(following, 1 - AY), lanes(v, 1))
        before = jnp.where(j_at == 0, lanes(preceding, AY - 1), lanes(v, -1))
        other = jnp.where(j_at % NP == NP - 1, after, jnp.where(j_at % NP == 0, before, v))
        return 0.5 * (v + other)

    def mean_rows(v, above, below):
        after = jnp.where(i_at == AX - 1, lanes(below, AY - n), lanes(v, AY))
        before = jnp.where(i_at == 0, lanes(above, n - AY), lanes(v, -AY))
        other = jnp.where(i_at % NP == NP - 1, after, jnp.where(i_at % NP == 0, before, v))
        return 0.5 * (v + other)

    for _ in range(2):
        across = [mean_columns(rate(v, own)) for v, own in zip(blocks, coefficients)]
        count = len(blocks)
        blocks = [
            blocks[b]
            + atmos_step
            * mean_rows(across[b], across[max(b - 1, 0)], across[min(b + 1, count - 1)])
            for b in range(count)
        ]
    return blocks


def prepare_kernel(
    sizes, first_ref, second_ref, h_ref, p_ref, w8_ref, tgt_ref, wgt_ref, rate_ref,
    ext_ref, mean_ref, left_ref, right_ref, high_ref, low_ref, weight_ref, row_ref, hot_ref,
):
    AX, AY, _, OX, OY, T, SLOT, H, nbh = sizes
    ks = SLOT // 128
    band = OX * OY // T
    rb = max(1, band // OY)
    static_fields = FIELDS - 1

    even = parity("comp") == 0
    from_up = chosen(even, second_ref, first_ref)
    from_dn = chosen(even, first_ref, second_ref)

    base = H * SENT + 2 * nbh * ks
    rates = [from_up(base, base + AY)] + [rate_ref[i] for i in range(AX)]
    rates.append(from_dn(base, base + AY))
    for i in range(-1, AX + 1):
        at = i + 1
        if i == -1 or i < AX and i % NP == NP - 1:
            value = 0.5 * (rates[at] + rates[at + 1])
        elif i % NP == 0:
            value = 0.5 * (rates[at] + rates[at - 1])
        else:
            value = rates[at]
        mean_ref[at] = value
    groups = (OX + 2 * H) // 8
    base = base + 4 * AY
    m = NP - 1
    up_edges, dn_edges = from_up(base, base + 8), from_dn(base, base + 8)
    for ref, j, lo in ((left_ref, 0, 0), (right_ref, AY - 1, m)):
        at = 8 * groups
        ref[at : at + AX + 2, :] = mean_ref[:, j, :]
        ref[at + AX + 2 : at + AX + 2 + m, :] = up_edges[lo : lo + m]
        ref[at + AX + 2 + m : at + AX + 2 + 2 * m, :] = dn_edges[lo : lo + m]

    base = H * SENT
    for k in range(ks):
        at = slice(128 * k, 128 * k + 128)
        t_lo, w_lo = base + k * nbh, base + (ks + k) * nbh
        for lo, count, target, weight in (
            (0, nbh, from_up(t_lo, t_lo + nbh), from_up(w_lo, w_lo + nbh)),
            (nbh, T, tgt_ref[0, :, at], wgt_ref[0, :, at]),
            (nbh + T, nbh, from_dn(t_lo, t_lo + nbh), from_dn(w_lo, w_lo + nbh)),
        ):
            target = target.astype(jnp.int32)
            weight_ref[lo : lo + count, at] = weight
            high_ref[lo : lo + count, at] = (target & (band - 1)) // LOW
            low_ref[lo : lo + count, at] = target & (LOW - 1)
            row_ref[lo : lo + count, at] = (target // OY) & (rb - 1)
            column = target & (OY - 1)
            edge = jnp.where(column < H, column, column - (OY - 2 * H))
            edge = jnp.where((column < H) | (column >= OY - H), edge, -1)
            for b in range(count):
                hot_ref[lo + b, :, at] = jnp.where(
                    edge[b : b + 1, :] == iota((2 * H, 128), 0), 1.0, 0.0
                ).astype(jnp.bfloat16)

    rows = OX + 2 * H

    def extended(f):
        own = h_ref[...] if f == 0 else p_ref[...] if f == 1 else w8_ref[f - 2]
        return jnp.concatenate(
            [from_up(H * f, H * f + H), own, from_dn(H * f, H * f + H)], axis=0
        )

    ext_ref[0] = extended(0)
    ext_ref[1] = extended(1)
    layers = {d: ocean_step * extended(2 + o) for o, d in enumerate(OFFSETS)}
    layers[0, 0] = -sum(layers[d] for d in OFFSETS)
    for o, d in enumerate(ALL_OFFSETS):
        ext_ref[2 + o] = pltpu.roll(layers[d], d[0] % rows, 0) if d[0] else layers[d]
    for g in range(groups):
        low = jnp.zeros((8, OY), jnp.float32)
        high = jnp.zeros((8, OY), jnp.float32)
        for f in range(static_fields):
            low, high = pack(low, high, ext_ref[f, 8 * g : 8 * g + 8, :], f, H)
        left_ref[8 * g : 8 * g + 8, :] = low
        right_ref[8 * g : 8 * g + 8, :] = high


def pack(low, high, block, f, H):
    count = block.shape[1] // H
    at = iota(block.shape, 1) // H
    low = jnp.where(at == (f + count // 2) % count, spin(block, H * (f + count // 2)), low)
    high = jnp.where(at == (f - 1) % count, spin(block, H * f), high)
    return low, high


def spin(value, shift):
    shift = shift % value.shape[1]
    return pltpu.roll(value, shift, 1) if shift else value


def remap_kernel(
    sizes, C, got_ref, weight_ref, row_ref, hot_ref, left_in, right_in,
    first_ref, second_ref, hi_s, mid_s, lo_s, edge_s,
):
    AX, AY, _, OX, OY, T, SLOT, H, nbh = sizes
    ks = SLOT // 128
    n = AX * AY
    NB = T + 2 * nbh
    band = OX * OY // T
    groups = (OX + 2 * H) // 8

    def row_of(k):
        return lax.rem(lax.axis_index("comp") + (k - 2) + C, C)

    def slot(c, lo, hi):
        return got_ref[pl.ds(pl.multiple_of(row_of(c) * T, T), T), lo:hi]

    blocks = [slot(k, SLOT, SLOT + n) for k in range(5)]
    winds = [
        (slot(k, SLOT + n, SLOT + 2 * n), slot(k, SLOT + 2 * n, SLOT + 3 * n))
        for k in range(5)
    ]
    final = surface_steps(blocks, winds, AX, AY)[1:4]

    for k in range(ks):
        at = slice(128 * k, 128 * k + 128)
        picked = [
            jnp.take_along_axis(
                final[b], slot(1 + b, 128 * k, 128 * k + 128).astype(jnp.int32), axis=1,
                mode="promise_in_bounds",
            )
            for b in range(3)
        ]
        for lo, count, value in (
            (0, nbh, picked[0][T - nbh :]),
            (nbh, T, picked[1]),
            (nbh + T, nbh, picked[2][:nbh]),
        ):
            product = weight_ref[lo : lo + count, at] * value
            hi = product.astype(jnp.bfloat16).astype(jnp.float32)
            rest = product - hi
            mid = rest.astype(jnp.bfloat16).astype(jnp.float32)
            hi_s[lo : lo + count, at] = hi
            mid_s[lo : lo + count, at] = mid
            lo_s[lo : lo + count, at] = rest - mid

    rb = max(1, band // OY)
    shared = max(1, OY // band)
    rows_at = iota((8, SLOT), 0)
    edge_s[...] = jnp.zeros(edge_s.shape, jnp.float32)
    for group in range(NB // shared):
        total = 0.0
        for b in range(group * shared, group * shared + shared):
            row = slice(b, b + 1)
            cell = row_ref[row, :] == rows_at
            left = jnp.concatenate(
                [jnp.where(cell, ref[row, :], 0.0) for ref in (hi_s, mid_s, lo_s)], axis=0
            ).astype(jnp.bfloat16)
            total = total + lax.dot_general(
                left, hot_ref[b], (((1,), (1,)), ((), ())), preferred_element_type=jnp.float32
            )
        edge_s[rb * group : rb * group + rb, : 2 * H] = (total[:8] + total[8:16] + total[16:])[:rb]

    f = FIELDS - 1
    even = parity("tile") == 0

    def put(rows, to_left, to_right):
        first_ref[rows, :] = jnp.where(even, to_right, to_left)
        second_ref[rows, :] = jnp.where(even, to_left, to_right)

    for g in range(groups):
        at = slice(8 * g, 8 * g + 8)
        block = edge_s[at, :]
        count = OY // H
        low_slot, high_slot = (f + count // 2) % count, (f - 1) % count
        slot_at = iota(block.shape, 1) // H
        put(
            at,
            jnp.where(slot_at == low_slot, spin(block, H * low_slot), left_in[at, :]),
            jnp.where(slot_at == high_slot, spin(block, H * (high_slot - 1)), right_in[at, :]),
        )
    at = slice(8 * groups, left_in.shape[0])
    put(at, left_in[at, :], right_in[at, :])


def subcycles(height, potential, push, layers):
    rows, width = height.shape
    for _ in range(SUBCYCLES):
        potential = (1.0 - friction) * potential + (ocean_step * wave_speed) * height + push
        shifted = {
            -1: pltpu.roll(potential, 1, 1),
            0: potential,
            1: pltpu.roll(potential, width - 1, 1),
        }
        part = {
            dr: sum(layers[dr, dc] * shifted[dc] for dc in (-1, 0, 1)) for dr in (-1, 0, 1)
        }
        height = height + part[0] + pltpu.roll(part[1], rows - 1, 0) + pltpu.roll(part[-1], 1, 0)
    return height, potential


def inner_kernel(
    sizes, ext_ref, high_ref, low_ref, hi_s, mid_s, lo_s, comp_first, comp_second, wind_ref,
    h_ref, p_ref, strip_ref, coef_ref, force_ref, placed_s,
):
    AX, AY, LEV, OX, OY, T, SLOT, H, nbh = sizes
    NB = T + 2 * nbh
    band = OX * OY // T

    count = band // LOW
    high_at = iota((count, SLOT), 0)
    low_at = iota((LOW, SLOT), 0)
    for b in range(NB):
        row = slice(b, b + 1)
        cell = high_ref[row, :] == high_at
        left = jnp.concatenate(
            [jnp.where(cell, ref[row, :], 0.0) for ref in (hi_s, mid_s, lo_s)], axis=0
        ).astype(jnp.bfloat16)
        hot = jnp.where(low_ref[row, :] == low_at, jnp.bfloat16(1.0), jnp.bfloat16(0.0))
        placed = lax.dot_general(
            left, hot, (((1,), (1,)), ((), ())), preferred_element_type=jnp.float32
        )
        placed_s[count * b : count * b + count, :LOW] = (
            placed[:count] + placed[count : 2 * count] + placed[2 * count :]
        )
    pieces = OY // LOW
    lane_piece = iota((OX + 2 * H, OY), 1) // LOW
    force = None
    for q in range(pieces):
        piece = spin(placed_s[pl.ds(q, OX + 2 * H, stride=pieces), :], LOW * q)
        force = piece if force is None else jnp.where(lane_piece == q, piece, force)
    force_ref[...] = force

    fields = [ext_ref[f] for f in range(FIELDS - 1)] + [force_ref[...]]
    lane = iota(fields[0].shape, 1)
    for f, field in enumerate(fields):
        strip_ref[f] = jnp.where(
            lane < 2 * H,
            field,
            jnp.where((lane >= OY // 2 - 2 * H) & (lane < OY // 2), spin(field, OY // 2), 0.0),
        )
    height, potential = subcycles(
        fields[0], fields[1], ocean_step * fields[-1],
        {d: fields[2 + o] for o, d in enumerate(ALL_OFFSETS)},
    )
    h_ref[...] = height[H : H + OX]
    p_ref[...] = potential[H : H + OX]

    even = parity("comp") == 0
    from_up = chosen(even, comp_second, comp_first)
    from_dn = chosen(even, comp_first, comp_second)
    base = H * SENT + 2 * nbh * (SLOT // 128) + 2 * AY
    first_c, second_c = column_coefficients(AY, LEV)
    for i in range(-1, AX + 1):
        if 0 <= i < AX:
            east, north = (wind_ref[m, i].astype(jnp.float32) for m in range(2))
            others = list(range(NP))
        else:
            side = from_up if i < 0 else from_dn
            east, north = (side(base + AY * m, base + AY * m + AY) for m in range(2))
            others = list(range(NP)) if i >= AX else list(range(NP))[::-1]
        for m, shift in enumerate(SHIFTS):
            coef_ref[i + 1, m] = viscosity * second_c[shift] - north * first_c[shift]
        for m, k in enumerate(others):
            field = viscosity * float(D2[i % NP, k]) - east * float(D1[i % NP, k])
            if k == i % NP:
                field = field + (viscosity * second_c[0] - north * first_c[0])
            coef_ref[i + 1, len(SHIFTS) + m] = field


def ocean_kernel(
    sizes, strip_ref, h_ref, p_ref, first_ref, second_ref, mean_ref, comp_first, comp_second,
    a_ref, coef_ref, src_ref,
    h_out, p_out, send_ref, next_ref, mean2_ref,
):
    AX, AY, LEV, OX, OY, T, SLOT, H, nbh = sizes
    ks = SLOT // 128
    rows = OX + 2 * H
    groups = rows // 8
    lane = iota((8, OY), 1)
    even = parity("tile") == 0
    left_side = chosen(even, second_ref, first_ref)
    right_side = chosen(even, first_ref, second_ref)
    even = parity("comp") == 0
    from_up = chosen(even, comp_second, comp_first)
    from_dn = chosen(even, comp_first, comp_second)

    odd_slot = (lane // H) % 2 == 1
    mixed = []
    for g in range(groups):
        left, right = left_side(8 * g, 8 * g + 8), right_side(8 * g, 8 * g + 8)
        mixed.append((jnp.where(odd_slot, left, right), jnp.where(odd_slot, right, left)))
    halo = (lane >= OY - H) | (lane >= OY // 2) & (lane < OY // 2 + H)
    fields = [
        jnp.concatenate(
            [
                jnp.where(
                    halo, spin(mixed[g][f % 2], -H * f), strip_ref[f, 8 * g : 8 * g + 8, :]
                )
                for g in range(groups)
            ],
            axis=0,
        )
        for f in range(FIELDS)
    ]
    edge_h, edge_p = subcycles(
        fields[0], fields[1], ocean_step * fields[-1],
        {d: fields[2 + o] for o, d in enumerate(ALL_OFFSETS)},
    )
    lane = iota((OX, OY), 1)

    def merge(inner, edge):
        edge = edge[H : H + OX]
        return jnp.where(
            lane < H, edge, jnp.where(lane >= OY - H, spin(edge, OY // 2), inner)
        )

    final = merge(h_ref[...], edge_h)
    h_out[...] = final
    p_out[...] = merge(p_ref[...], edge_p)

    band = OX * OY // T
    rb = max(1, band // OY)
    source = src_ref[...]
    operands = []
    for r in range(rb):
        operands.append(
            jnp.concatenate(
                [final[(q * band) // OY + r : (q * band) // OY + r + 1, :] for q in range(T)], axis=0
            )
        )
    for k in range(ks):
        index = source[:, 128 * k : 128 * k + 128]
        lanes_at = index & (OY - 1)
        row_at = (index // OY) & (rb - 1)
        value = None
        for r in range(rb):
            got = jnp.take_along_axis(operands[r], lanes_at, axis=1, mode="promise_in_bounds")
            value = got if value is None else jnp.where(row_at == r, got, value)
        for q in range(T):
            send_ref[q, AX + k : AX + k + 1, :] = value[q : q + 1, :]

    base = H * SENT + 2 * nbh * ks
    at = 8 * groups
    rims_left = left_side(at, at + AX + 2 * NP)
    rims_right = right_side(at, at + AX + 2 * NP)
    column_at = iota((AY, LEV), 0)

    def advance(i, before):
        at = i + 1
        return before + atmos_step * column_mean(
            mean_ref[at], rims_left[at : at + 1, :], rims_right[at : at + 1, :]
        )

    def tendency(i, row, others):
        along = [coef_ref[i + 1, m] * column_shift(row, s) for m, s in enumerate(SHIFTS)]
        across = [coef_ref[i + 1, len(SHIFTS) + m] * v for m, v in enumerate(others)]
        return sum_pairs(along + across)

    state = [advance(i, a_ref[i]) for i in range(AX)]
    rates = {}
    for i in range(AX):
        next_ref[i] = state[i]
        start = i - i % NP
        rates[i] = tendency(i, state[i], state[start : start + NP])
    for i, side, lo in ((-1, from_up, AX + 2), (AX, from_dn, AX + 1 + NP)):
        rim = advance(i, 0.0)
        edges = [
            (0.5 * atmos_step)
            * jnp.where(
                column_at == 0,
                rims_left[at : at + 1, :],
                jnp.where(column_at == AY - 1, rims_right[at : at + 1, :], 0.0),
            )
            for at in range(lo, lo + NP - 1)
        ]
        rates[i] = side(base + AY, base + 2 * AY) + tendency(i, rim, [rim] + edges)
    for i in range(AX):
        if i % NP == NP - 1:
            value = 0.5 * (rates[i] + rates[i + 1])
        elif i % NP == 0:
            value = 0.5 * (rates[i] + rates[i - 1])
        else:
            value = rates[i]
        mean2_ref[i] = value
    left_edge = mean2_ref[:, 0, :]
    right_edge = mean2_ref[:, AY - 1, :]
    for q in range(T):
        send_ref[q, :AX, :] = jnp.where(
            beside(T, 1) == q, right_edge, jnp.where(beside(T, -1) == q, left_edge, 0.0)
        )


def final_kernel(
    sizes, got_ref, next_ref, mean2_ref, h_ref, p_ref, tgt_ref, wgt_ref,
    a_dst, h_dst, p_dst, flux_dst, a_out, flux_out, sems,
):
    AX, AY, _, _, _, T, SLOT, _, _ = sizes
    copies = [
        pltpu.make_async_copy(source, target, sems.at[k])
        for k, (source, target) in enumerate(
            ((h_ref, h_dst), (p_ref, p_dst), (a_out, a_dst), (flux_out, flux_dst))
        )
    ]
    copies[0].start()
    copies[1].start()
    ks = SLOT // 128
    points = AX * AY // T
    left = got_ref[beside(T, -1), :AX, :]
    right = got_ref[beside(T, 1), :AX, :]
    for i in range(AX):
        a_out[i] = next_ref[i] + atmos_step * column_mean(
            mean2_ref[i], left[i : i + 1], right[i : i + 1]
        )
    copies[2].start()
    base = iota((T, 128), 0) * points
    totals = [jnp.zeros((T, 128), jnp.float32) for _ in range(points)]
    for k in range(ks):
        value = jnp.concatenate([got_ref[q, AX + k : AX + k + 1, :] for q in range(T)], axis=0)
        product = wgt_ref[:, 128 * k : 128 * k + 128] * value
        local = tgt_ref[:, 128 * k : 128 * k + 128] - base
        for m in range(points):
            totals[m] = totals[m] + jnp.where(local == m, product, 0.0)
    for m in range(points):
        flux_out[:, m : m + 1] = jnp.sum(totals[m], axis=1, keepdims=True)
    copies[3].start()
    for copy in copies:
        copy.wait()


def meeting(count, start):
    pairs = []
    for low in range(start, count + start, 2):
        pairs += [(low % count, (low + 1) % count), ((low + 1) % count, low % count)]
    return pairs


def on_device(C, T, *arguments):
    return step(C, T, *arguments)


def step(
    C, T,
    atmos_state, wind_field, ocean_height, ocean_potential, ocean_neighbors, ocean_coupling,
    downward_source, downward_target, downward_weight, upward_source, upward_target, upward_weight,
):
    AX, AY, LEV = atmos_state.shape
    OX, OY = ocean_height.shape
    SLOT = downward_source.shape[-1]
    H = SUBCYCLES
    n = AX * AY
    band = OX * OY // T
    nbh = H * OY // band
    ks = SLOT // 128
    sizes = (AX, AY, LEV, OX, OY, T, SLOT, H, nbh)
    f32, i32 = jnp.float32, jnp.int32
    static_rows = H * SENT + 2 * nbh * ks + 4 * AY + 8
    front_args = (
        downward_source, atmos_state, wind_field, ocean_neighbors, ocean_coupling,
        ocean_height, ocean_potential, downward_target, downward_weight,
    )
    front_outs = [
        ((C * T, 1, SLOT + 3 * n), f32), ((static_rows, 128), f32), ((static_rows, 128), f32),
        ((FIELDS - 4, OX, OY), f32), ((AX, AY, LEV), f32),
    ]
    slots, comp_first, comp_second, w8, rate = call(
        functools.partial(front_kernel, sizes, C),
        front_outs,
        front_args,
        scratch=[pltpu.VMEM(v.shape, v.dtype) for v in front_args]
        + [pltpu.VMEM(*v) for v in front_outs]
        + [pltpu.SemaphoreType.DMA((14,))],
        raw_in=True,
        raw_out=5,
        limit=None,
    )
    comp_second = lax.ppermute(comp_second, "comp", meeting(C, 1))
    comp_first = lax.ppermute(comp_first, "comp", meeting(C, 0))
    got = lax.all_to_all(slots, ("comp", "tile"), 0, 0, tiled=True)
    got = got.reshape(C * T, SLOT + 3 * n)

    edge_rows = OX + 2 * H + AX + 2 * NP
    NB = T + 2 * nbh
    ext, mean, left, right, high, low, weight, row, hot = call(
        functools.partial(prepare_kernel, sizes),
        [((FIELDS - 1, OX + 2 * H, OY), f32), ((AX + 2, AY, LEV), f32)]
        + [((edge_rows, 128), f32)] * 2
        + [((NB, SLOT), i32)] * 2
        + [((NB, SLOT), f32), ((NB, SLOT), i32), ((NB, 2 * H, SLOT), jnp.bfloat16)],
        (
            comp_first, comp_second, ocean_height, ocean_potential, w8,
            downward_target, downward_weight, rate,
        ),
    )
    tile_first, tile_second, part_hi, part_mid, part_lo = call(
        functools.partial(remap_kernel, sizes, C),
        [((edge_rows, 128), f32)] * 2 + [((NB, SLOT), f32)] * 3,
        (got, weight, row, hot, left, right),
        scratch=[pltpu.VMEM((OX + 2 * H, OY), f32)],
    )
    tile_second = lax.ppermute(tile_second, "tile", meeting(T, 1))
    tile_first = lax.ppermute(tile_first, "tile", meeting(T, 0))

    inner_h, inner_p, strips, coef = call(
        functools.partial(inner_kernel, sizes),
        [((OX, OY), f32)] * 2
        + [((FIELDS, OX + 2 * H, OY), f32), ((AX + 2, len(SHIFTS) + NP, AY, LEV), f32)],
        (ext, high, low, part_hi, part_mid, part_lo, comp_first, comp_second, wind_field),
        scratch=[pltpu.VMEM((OX + 2 * H, OY), f32), pltpu.VMEM((NB * band // LOW, OY), f32)],
    )
    height, potential, send, state, mean2 = call(
        functools.partial(ocean_kernel, sizes),
        [((OX, OY), f32)] * 2 + [((T, AX + max(8, ks), 128), f32)] + [((AX, AY, LEV), f32)] * 2,
        (
            strips, inner_h, inner_p, tile_first, tile_second, mean, comp_first, comp_second,
            atmos_state, coef, upward_source[0],
        ),
    )
    back = lax.all_to_all(send, "tile", 0, 0, tiled=True)
    atmos, height, potential, flux = call(
        functools.partial(final_kernel, sizes),
        [((AX, AY, LEV), f32)] + [((OX, OY), f32)] * 2 + [((T, n // T), f32)],
        (back, state, mean2, height, potential, upward_target[0], upward_weight[0]),
        scratch=[
            pltpu.VMEM((AX, AY, LEV), f32),
            pltpu.VMEM((T, n // T), f32),
            pltpu.SemaphoreType.DMA((4,)),
        ],
        raw_out=4,
    )
    return (atmos, height, potential, flux.reshape(AX, AY))


def solution(mesh):
    return jax.shard_map(
        functools.partial(on_device, mesh.shape["comp"], mesh.shape["tile"]),
        mesh=mesh,
        in_specs=(
            P("comp", "tile", None),
            P(None, "comp", "tile", None),
            P("comp", "tile"),
            P("comp", "tile"),
            P(None, "comp", "tile"),
            P(None, "comp", "tile"),
            P("comp", "tile", None),
            P("comp", "tile", None),
            P("comp", "tile", None),
            P("comp", "tile", None),
            P("comp", "tile", None),
            P("comp", "tile", None),
        ),
        out_specs=(
            P("comp", "tile", None),
            P("comp", "tile"),
            P("comp", "tile"),
            P("comp", "tile"),
        ),
        check_vma=False,
    )
```

```python
import functools

import jax
import jax.numpy as jnp
import numpy as np
from jax import lax
from jax.experimental import pallas as pl
from jax.experimental.pallas import tpu as pltpu
from jax.sharding import PartitionSpec as P

NP = 4
SUBCYCLES = 8

atmos_step = 0.05
viscosity = 0.05
ocean_step = 0.2
wave_speed = 1.0
friction = 0.05

OFFSETS = [(a, b) for a in (-1, 0, 1) for b in (-1, 0, 1) if (a, b) != (0, 0)]
ALL_OFFSETS = [(a, b) for a in (-1, 0, 1) for b in (-1, 0, 1)]
SENT = 2 + len(OFFSETS)
FIELDS = 3 + len(ALL_OFFSETS)
LOW = 32
SHIFTS = [s for s in range(1 - NP, NP) if s]


def gll_derivative():
    points = np.array([-1.0, -1.0 / np.sqrt(5.0), 1.0 / np.sqrt(5.0), 1.0])
    weights = np.array(
        [1.0 / np.prod([points[j] - points[k] for k in range(4) if k != j]) for j in range(4)]
    )
    matrix = np.zeros((4, 4))
    for i in range(4):
        for j in range(4):
            if i != j:
                matrix[i, j] = weights[j] / weights[i] / (points[i] - points[j])
        matrix[i, i] = -np.sum(matrix[i])
    return matrix


D1 = gll_derivative()
D2 = D1 @ D1


def band_coefficients(position, matrix):
    result = {}
    for shift in range(1 - NP, NP):
        value = jnp.zeros(position.shape, jnp.float32)
        for i in range(NP):
            if 0 <= i + shift < NP:
                value = jnp.where(position == i, float(matrix[i, i + shift]), value)
        result[shift] = value
    return result


def sum_pairs(terms):
    while len(terms) > 1:
        terms = [sum(terms[k : k + 2][1:], terms[k]) for k in range(0, len(terms), 2)]
    return terms[0]


def iota(shape, dim):
    return lax.broadcasted_iota(jnp.int32, shape, dim)


def full_specs(count):
    return [pl.BlockSpec(memory_space=pltpu.VMEM) for _ in range(count)]


def call(body, out_shapes, args, scratch=(), raw_in=False, raw_out=0, limit=16):
    raw = pl.BlockSpec(memory_space=pltpu.HBM)
    return pl.pallas_call(
        body,
        out_shape=[jax.ShapeDtypeStruct(s, d) for s, d in out_shapes],
        in_specs=([raw] * len(args) if raw_in else full_specs(len(args))),
        out_specs=[raw] * raw_out + full_specs(len(out_shapes) - raw_out),
        scratch_shapes=list(scratch),
        compiler_params=pltpu.CompilerParams(
            vmem_limit_bytes=limit * 1024 * 1024 if limit else None
        ),
        cost_estimate=pl.CostEstimate(
            flops=1000000, bytes_accessed=1000000, transcendentals=0
        ),
    )(*args)


def column_shift(row, shift):
    extent, levels = row.shape
    tiles = row.reshape(extent // 8, 8, levels)
    return pltpu.roll(tiles, (-shift) % 8, 1).reshape(extent, levels)


def second_terms(row, first_c, second_c):
    slope = first_c[0] * row
    curve = second_c[0] * row
    for shift in range(1 - NP, NP):
        if shift:
            moved = column_shift(row, shift)
            slope = slope + first_c[shift] * moved
            curve = curve + second_c[shift] * moved
    return slope, curve


def row_rate(element, position, wind_east, wind_north, first_c, second_c):
    slope_east = sum(float(D1[position, k]) * element[k] for k in range(NP))
    curve_east = sum(float(D2[position, k]) * element[k] for k in range(NP))
    slope_north, curve_north = second_terms(element[position], first_c, second_c)
    return viscosity * (curve_east + curve_north) - (
        wind_east * slope_east + wind_north * slope_north
    )


def column_mean(row, left_edge, right_edge):
    extent, levels = row.shape
    at = iota((extent, levels), 0)
    after = jnp.where(at == extent - 1, right_edge, pltpu.roll(row, extent - 1, 0))
    before = jnp.where(at == 0, left_edge, pltpu.roll(row, 1, 0))
    position = at % NP
    other = jnp.where(position == NP - 1, after, jnp.where(position == 0, before, row))
    return 0.5 * (row + other)


def column_coefficients(extent, levels):
    position = iota((extent, levels), 0) % NP
    return band_coefficients(position, D1), band_coefficients(position, D2)


def front_kernel(sizes, C, *refs):
    AX, AY, LEV, OX, OY, T, SLOT, H, nbh = sizes
    ks = SLOT // 128
    n = AX * AY
    inputs, outputs, held, made, sems = refs[:9], refs[9:14], refs[14:23], refs[23:28], refs[28]
    loads = [pltpu.make_async_copy(inputs[k], held[k], sems.at[k]) for k in range(9)]
    stores = [pltpu.make_async_copy(made[k], outputs[k], sems.at[9 + k]) for k in range(5)]
    for copy in loads:
        copy.start()
    src_ref, a_ref, wind_ref, nbr_ref, cpl_ref, h_ref, p_ref, tgt_ref, wgt_ref = held
    slots_ref, first_ref, second_ref, w8_ref, rate_ref = made
    for copy in loads[:3]:
        copy.wait()
    source = src_ref[0].astype(jnp.float32)
    surface = [
        jnp.transpose(v.astype(jnp.float32).reshape(n, LEV))[LEV - 1 :, :]
        for v in (a_ref[...], wind_ref[0], wind_ref[1])
    ]

    def spread(c, carry):
        for q in range(T):
            at = c * T + q
            slots_ref[at, :, :SLOT] = source[q : q + 1, :]
            for m in range(3):
                slots_ref[at, :, SLOT + n * m : SLOT + n * m + n] = surface[m]
        return carry

    if C <= 4:
        for c in range(C):
            spread(c, 0)
    else:
        lax.fori_loop(0, C, spread, 0)
    stores[0].start()

    even = parity("comp") == 0

    def put(at, to_up, to_dn):
        rows = slice(at, at + to_up.shape[0])
        first_ref[rows, :] = jnp.where(even, to_dn, to_up)
        second_ref[rows, :] = jnp.where(even, to_up, to_dn)

    first_c, second_c = column_coefficients(AY, LEV)
    rates = []
    for i in range(AX):
        start = i - i % NP
        element = [a_ref[start + k] for k in range(NP)]
        rates.append(
            row_rate(
                element,
                i % NP,
                wind_ref[0, i].astype(jnp.float32),
                wind_ref[1, i].astype(jnp.float32),
                first_c,
                second_c,
            )
        )
        rate_ref[i] = rates[i]
    stores[4].start()
    none = jnp.zeros((1, LEV), jnp.float32)
    sides = []
    for rim, step in ((0, 1), (AX - 1, -1)):
        at_rim = rim % NP
        east, north = (wind_ref[m, rim].astype(jnp.float32) for m in range(2))
        others, partial = [], 0.0
        for d in range(1, NP):
            i = rim + step * d
            mean = 0.5 * (rates[i] + rates[i + step]) if d == NP - 1 else rates[i]
            others.append(mean)
            state = a_ref[i] + atmos_step * column_mean(mean, none, none)
            at_i = i % NP
            partial = partial + (
                viscosity * float(D2[at_rim, at_i]) - east * float(D1[at_rim, at_i])
            ) * state
        edges = jnp.concatenate(
            [v[:1] for v in others] + [v[AY - 1 :] for v in others] + [none] * 2, axis=0
        )
        own = a_ref[rim]
        slope, curve = second_terms(own, first_c, second_c)
        partial = (
            partial
            + viscosity * (float(D2[at_rim, at_rim]) * own + curve)
            - (east * (float(D1[at_rim, at_rim]) * own) + north * slope)
        )
        sides.append([rates[rim], partial, east, north, edges])
    at = H * SENT + 2 * nbh * ks
    for to_up, to_dn in zip(*sides):
        put(at, to_up, to_dn)
        at += to_up.shape[0]

    for copy in loads[3:]:
        copy.wait()

    def weights(lo, hi):
        centre = (iota((hi - lo, OY), 0) + lo + 1) * (OY + 2) + iota((hi - lo, OY), 1) + 1
        offset = [nbr_ref[l, lo:hi, :] - centre for l in range(6)]
        coupling = [cpl_ref[l, lo:hi, :] for l in range(6)]
        result = []
        for o, (dr, dc) in enumerate(OFFSETS):
            code = dr * (OY + 2) + dc
            terms = [jnp.where(offset[l] == code, coupling[l], 0.0) for l in range(6)]
            result.append(sum_pairs(terms))
            w8_ref[o, lo:hi, :] = result[o]
        return result

    top, bottom = weights(0, H), weights(OX - H, OX)
    for f, field in enumerate((h_ref, p_ref)):
        put(H * f, field[:H, :], field[OX - H :, :])
    for o in range(len(OFFSETS)):
        put(H * (2 + o), top[o], bottom[o])
    at = H * SENT
    for ref in (tgt_ref, wgt_ref):
        table = ref[0].astype(jnp.float32)
        for k in range(ks):
            chunk = table[:, 128 * k : 128 * k + 128]
            put(at, chunk[:nbh], chunk[T - nbh :])
            at += nbh
    stores[1].start()
    stores[2].start()
    if OX > 2 * H:
        weights(H, OX - H)
    stores[3].start()
    for copy in stores:
        copy.wait()


def parity(axis):
    return lax.rem(lax.axis_index(axis), 2)


def beside(count, step):
    return lax.rem(lax.axis_index("tile") + step + count, count)


def chosen(flag, one, other):
    return lambda lo, hi: jnp.where(flag, one[lo:hi, :], other[lo:hi, :])


def surface_coefficients(shape, stride, matrix):
    return band_coefficients((iota(shape, 1) // stride) % NP, matrix)


def surface_steps(blocks, winds, AX, AY):
    shape = blocks[0].shape
    n = AX * AY
    lane = iota(shape, 1)
    i_at, j_at = lane // AY, lane % AY
    x1 = surface_coefficients(shape, AY, D1)
    x2 = surface_coefficients(shape, AY, D2)
    y1 = surface_coefficients(shape, 1, D1)
    y2 = surface_coefficients(shape, 1, D2)

    def lanes(v, shift):
        return pltpu.roll(v, (-shift) % n, 1) if shift % n else v

    coefficients = []
    for east, north in winds:
        own = {(0, 0): viscosity * (x2[0] + y2[0]) - (east * x1[0] + north * y1[0])}
        for s in SHIFTS:
            own[s, 0] = viscosity * x2[s] - east * x1[s]
            own[0, s] = viscosity * y2[s] - north * y1[s]
        coefficients.append(own)

    def rate(v, own):
        return sum_pairs([field * lanes(v, s * AY + r) for (s, r), field in own.items()])

    def mean_columns(v):
        devices = shape[0]
        following = pltpu.roll(v, devices - 1, 0)
        preceding = pltpu.roll(v, 1, 0)
        after = jnp.where(j_at == AY - 1, lanes(following, 1 - AY), lanes(v, 1))
        before = jnp.where(j_at == 0, lanes(preceding, AY - 1), lanes(v, -1))
        other = jnp.where(j_at % NP == NP - 1, after, jnp.where(j_at % NP == 0, before, v))
        return 0.5 * (v + other)

    def mean_rows(v, above, below):
        after = jnp.where(i_at == AX - 1, lanes(below, AY - n), lanes(v, AY))
        before = jnp.where(i_at == 0, lanes(above, n - AY), lanes(v, -AY))
        other = jnp.where(i_at % NP == NP - 1, after, jnp.where(i_at % NP == 0, before, v))
        return 0.5 * (v + other)

    for _ in range(2):
        rates = [rate(v, own) for v, own in zip(blocks, coefficients)]
        count = len(blocks)
        blocks = [
            blocks[b]
            + atmos_step
            * mean_columns(
                mean_rows(rates[b], rates[max(b - 1, 0)], rates[min(b + 1, count - 1)])
            )
            for b in range(count)
        ]
    return blocks


def prepare_kernel(
    sizes, first_ref, second_ref, h_ref, p_ref, w8_ref, tgt_ref, wgt_ref, rate_ref,
    ext_ref, mean_ref, left_ref, right_ref, high_ref, low_ref, weight_ref, row_ref, hot_ref,
):
    AX, AY, _, OX, OY, T, SLOT, H, nbh = sizes
    ks = SLOT // 128
    band = OX * OY // T
    rb = max(1, band // OY)
    static_fields = FIELDS - 1

    even = parity("comp") == 0
    from_up = chosen(even, second_ref, first_ref)
    from_dn = chosen(even, first_ref, second_ref)

    base = H * SENT + 2 * nbh * ks
    rates = [from_up(base, base + AY)] + [rate_ref[i] for i in range(AX)]
    rates.append(from_dn(base, base + AY))
    for i in range(-1, AX + 1):
        at = i + 1
        if i == -1 or i < AX and i % NP == NP - 1:
            value = 0.5 * (rates[at] + rates[at + 1])
        elif i % NP == 0:
            value = 0.5 * (rates[at] + rates[at - 1])
        else:
            value = rates[at]
        mean_ref[at] = value
    groups = (OX + 2 * H) // 8
    base = base + 4 * AY
    m = NP - 1
    up_edges, dn_edges = from_up(base, base + 8), from_dn(base, base + 8)
    for ref, j, lo in ((left_ref, 0, 0), (right_ref, AY - 1, m)):
        at = 8 * groups
        ref[at : at + AX + 2, :] = mean_ref[:, j, :]
        ref[at + AX + 2 : at + AX + 2 + m, :] = up_edges[lo : lo + m]
        ref[at + AX + 2 + m : at + AX + 2 + 2 * m, :] = dn_edges[lo : lo + m]

    base = H * SENT
    for k in range(ks):
        at = slice(128 * k, 128 * k + 128)
        t_lo, w_lo = base + k * nbh, base + (ks + k) * nbh
        for lo, count, target, weight in (
            (0, nbh, from_up(t_lo, t_lo + nbh), from_up(w_lo, w_lo + nbh)),
            (nbh, T, tgt_ref[0, :, at], wgt_ref[0, :, at]),
            (nbh + T, nbh, from_dn(t_lo, t_lo + nbh), from_dn(w_lo, w_lo + nbh)),
        ):
            target = target.astype(jnp.int32)
            weight_ref[lo : lo + count, at] = weight
            high_ref[lo : lo + count, at] = (target & (band - 1)) // LOW
            low_ref[lo : lo + count, at] = target & (LOW - 1)
            row_ref[lo : lo + count, at] = (target // OY) & (rb - 1)
            column = target & (OY - 1)
            edge = jnp.where(column < H, column, column - (OY - 2 * H))
            edge = jnp.where((column < H) | (column >= OY - H), edge, -1)
            for b in range(count):
                hot_ref[lo + b, :, at] = jnp.where(
                    edge[b : b + 1, :] == iota((2 * H, 128), 0), 1.0, 0.0
                ).astype(jnp.bfloat16)

    rows = OX + 2 * H

    def extended(f):
        own = h_ref[...] if f == 0 else p_ref[...] if f == 1 else w8_ref[f - 2]
        return jnp.concatenate(
            [from_up(H * f, H * f + H), own, from_dn(H * f, H * f + H)], axis=0
        )

    ext_ref[0] = extended(0)
    ext_ref[1] = extended(1)
    layers = {d: ocean_step * extended(2 + o) for o, d in enumerate(OFFSETS)}
    layers[0, 0] = -sum(layers[d] for d in OFFSETS)
    for o, d in enumerate(ALL_OFFSETS):
        ext_ref[2 + o] = pltpu.roll(layers[d], d[0] % rows, 0) if d[0] else layers[d]
    for g in range(groups):
        low = jnp.zeros((8, OY), jnp.float32)
        high = jnp.zeros((8, OY), jnp.float32)
        for f in range(static_fields):
            low, high = pack(low, high, ext_ref[f, 8 * g : 8 * g + 8, :], f, H)
        left_ref[8 * g : 8 * g + 8, :] = low
        right_ref[8 * g : 8 * g + 8, :] = high


def pack(low, high, block, f, H):
    count = block.shape[1] // H
    at = iota(block.shape, 1) // H
    low = jnp.where(at == (f + count // 2) % count, spin(block, H * (f + count // 2)), low)
    high = jnp.where(at == (f - 1) % count, spin(block, H * f), high)
    return low, high


def spin(value, shift):
    shift = shift % value.shape[1]
    return pltpu.roll(value, shift, 1) if shift else value


def remap_kernel(
    sizes, C, got_ref, weight_ref, row_ref, hot_ref, left_in, right_in,
    first_ref, second_ref, hi_s, mid_s, lo_s, edge_s,
):
    AX, AY, _, OX, OY, T, SLOT, H, nbh = sizes
    ks = SLOT // 128
    n = AX * AY
    NB = T + 2 * nbh
    band = OX * OY // T
    groups = (OX + 2 * H) // 8

    def row_of(k):
        return lax.rem(lax.axis_index("comp") + (k - 2) + C, C)

    def slot(c, lo, hi):
        return got_ref[pl.ds(pl.multiple_of(row_of(c) * T, T), T), lo:hi]

    blocks = [slot(k, SLOT, SLOT + n) for k in range(5)]
    winds = [
        (slot(k, SLOT + n, SLOT + 2 * n), slot(k, SLOT + 2 * n, SLOT + 3 * n))
        for k in range(5)
    ]
    final = surface_steps(blocks, winds, AX, AY)[1:4]

    for k in range(ks):
        at = slice(128 * k, 128 * k + 128)
        picked = [
            jnp.take_along_axis(
                final[b], slot(1 + b, 128 * k, 128 * k + 128).astype(jnp.int32), axis=1,
                mode="promise_in_bounds",
            )
            for b in range(3)
        ]
        for lo, count, value in (
            (0, nbh, picked[0][T - nbh :]),
            (nbh, T, picked[1]),
            (nbh + T, nbh, picked[2][:nbh]),
        ):
            product = weight_ref[lo : lo + count, at] * value
            hi = product.astype(jnp.bfloat16).astype(jnp.float32)
            rest = product - hi
            mid = rest.astype(jnp.bfloat16).astype(jnp.float32)
            hi_s[lo : lo + count, at] = hi
            mid_s[lo : lo + count, at] = mid
            lo_s[lo : lo + count, at] = rest - mid

    rb = max(1, band // OY)
    shared = max(1, OY // band)
    rows_at = iota((8, SLOT), 0)
    for group in range(NB // shared):
        total = 0.0
        for b in range(group * shared, group * shared + shared):
            row = slice(b, b + 1)
            cell = row_ref[row, :] == rows_at
            left = jnp.concatenate(
                [jnp.where(cell, ref[row, :], 0.0) for ref in (hi_s, mid_s, lo_s)], axis=0
            ).astype(jnp.bfloat16)
            total = total + lax.dot_general(
                left, hot_ref[b], (((1,), (1,)), ((), ())), preferred_element_type=jnp.float32
            )
        edge_s[rb * group : rb * group + rb, : 2 * H] = (total[:8] + total[8:16] + total[16:])[:rb]

    f = FIELDS - 1
    even = parity("tile") == 0

    def put(rows, to_left, to_right):
        first_ref[rows, :] = jnp.where(even, to_right, to_left)
        second_ref[rows, :] = jnp.where(even, to_left, to_right)

    for g in range(groups):
        at = slice(8 * g, 8 * g + 8)
        block = edge_s[at, :]
        count = OY // H
        low_slot, high_slot = (f + count // 2) % count, (f - 1) % count
        slot_at = iota(block.shape, 1) // H
        put(
            at,
            jnp.where(slot_at == low_slot, spin(block, H * low_slot), left_in[at, :]),
            jnp.where(slot_at == high_slot, spin(block, H * (high_slot - 1)), right_in[at, :]),
        )
    at = slice(8 * groups, left_in.shape[0])
    put(at, left_in[at, :], right_in[at, :])


def subcycles(height, potential, push, layers):
    rows, width = height.shape
    for _ in range(SUBCYCLES):
        potential = (1.0 - friction) * potential + (ocean_step * wave_speed) * height + push
        shifted = {
            -1: pltpu.roll(potential, 1, 1),
            0: potential,
            1: pltpu.roll(potential, width - 1, 1),
        }
        part = {
            dr: sum(layers[dr, dc] * shifted[dc] for dc in (-1, 0, 1)) for dr in (-1, 0, 1)
        }
        height = height + part[0] + pltpu.roll(part[1], rows - 1, 0) + pltpu.roll(part[-1], 1, 0)
    return height, potential


def inner_kernel(
    sizes, ext_ref, high_ref, low_ref, hi_s, mid_s, lo_s, comp_first, comp_second, wind_ref,
    h_ref, p_ref, strip_ref, coef_ref, force_ref, placed_s,
):
    AX, AY, LEV, OX, OY, T, SLOT, H, nbh = sizes
    NB = T + 2 * nbh
    band = OX * OY // T

    count = band // LOW
    high_at = iota((count, SLOT), 0)
    low_at = iota((LOW, SLOT), 0)
    for b in range(NB):
        row = slice(b, b + 1)
        cell = high_ref[row, :] == high_at
        left = jnp.concatenate(
            [jnp.where(cell, ref[row, :], 0.0) for ref in (hi_s, mid_s, lo_s)], axis=0
        ).astype(jnp.bfloat16)
        hot = jnp.where(low_ref[row, :] == low_at, jnp.bfloat16(1.0), jnp.bfloat16(0.0))
        placed = lax.dot_general(
            left, hot, (((1,), (1,)), ((), ())), preferred_element_type=jnp.float32
        )
        placed_s[count * b : count * b + count, :LOW] = (
            placed[:count] + placed[count : 2 * count] + placed[2 * count :]
        )
    pieces = OY // LOW
    lane_piece = iota((OX + 2 * H, OY), 1) // LOW
    force = None
    for q in range(pieces):
        piece = spin(placed_s[pl.ds(q, OX + 2 * H, stride=pieces), :], LOW * q)
        force = piece if force is None else jnp.where(lane_piece == q, piece, force)
    force_ref[...] = force

    fields = [ext_ref[f] for f in range(FIELDS - 1)] + [force_ref[...]]
    lane = iota(fields[0].shape, 1)
    for f, field in enumerate(fields):
        strip_ref[f] = jnp.where(
            lane < 2 * H,
            field,
            jnp.where((lane >= OY // 2 - 2 * H) & (lane < OY // 2), spin(field, OY // 2), 0.0),
        )
    height, potential = subcycles(
        fields[0], fields[1], ocean_step * fields[-1],
        {d: fields[2 + o] for o, d in enumerate(ALL_OFFSETS)},
    )
    h_ref[...] = height[H : H + OX]
    p_ref[...] = potential[H : H + OX]

    even = parity("comp") == 0
    from_up = chosen(even, comp_second, comp_first)
    from_dn = chosen(even, comp_first, comp_second)
    base = H * SENT + 2 * nbh * (SLOT // 128) + 2 * AY
    first_c, second_c = column_coefficients(AY, LEV)
    for i in range(-1, AX + 1):
        if 0 <= i < AX:
            east, north = (wind_ref[m, i].astype(jnp.float32) for m in range(2))
            others = list(range(NP))
        else:
            side = from_up if i < 0 else from_dn
            east, north = (side(base + AY * m, base + AY * m + AY) for m in range(2))
            others = list(range(NP)) if i >= AX else list(range(NP))[::-1]
        for m, shift in enumerate(SHIFTS):
            coef_ref[i + 1, m] = viscosity * second_c[shift] - north * first_c[shift]
        for m, k in enumerate(others):
            field = viscosity * float(D2[i % NP, k]) - east * float(D1[i % NP, k])
            if k == i % NP:
                field = field + (viscosity * second_c[0] - north * first_c[0])
            coef_ref[i + 1, len(SHIFTS) + m] = field


def ocean_kernel(
    sizes, strip_ref, h_ref, p_ref, first_ref, second_ref, mean_ref, comp_first, comp_second,
    a_ref, coef_ref, src_ref,
    h_out, p_out, send_ref, next_ref, mean2_ref,
):
    AX, AY, LEV, OX, OY, T, SLOT, H, nbh = sizes
    ks = SLOT // 128
    rows = OX + 2 * H
    groups = rows // 8
    lane = iota((8, OY), 1)
    even = parity("tile") == 0
    left_side = chosen(even, second_ref, first_ref)
    right_side = chosen(even, first_ref, second_ref)
    even = parity("comp") == 0
    from_up = chosen(even, comp_second, comp_first)
    from_dn = chosen(even, comp_first, comp_second)

    odd_slot = (lane // H) % 2 == 1
    mixed = []
    for g in range(groups):
        left, right = left_side(8 * g, 8 * g + 8), right_side(8 * g, 8 * g + 8)
        mixed.append((jnp.where(odd_slot, left, right), jnp.where(odd_slot, right, left)))
    halo = (lane >= OY - H) | (lane >= OY // 2) & (lane < OY // 2 + H)
    fields = [
        jnp.concatenate(
            [
                jnp.where(
                    halo, spin(mixed[g][f % 2], -H * f), strip_ref[f, 8 * g : 8 * g + 8, :]
                )
                for g in range(groups)
            ],
            axis=0,
        )
        for f in range(FIELDS)
    ]
    edge_h, edge_p = subcycles(
        fields[0], fields[1], ocean_step * fields[-1],
        {d: fields[2 + o] for o, d in enumerate(ALL_OFFSETS)},
    )
    lane = iota((OX, OY), 1)

    def merge(inner, edge):
        edge = edge[H : H + OX]
        return jnp.where(
            lane < H, edge, jnp.where(lane >= OY - H, spin(edge, OY // 2), inner)
        )

    final = merge(h_ref[...], edge_h)
    h_out[...] = final
    p_out[...] = merge(p_ref[...], edge_p)

    band = OX * OY // T
    rb = max(1, band // OY)
    source = src_ref[...]
    operands = []
    for r in range(rb):
        operands.append(
            jnp.concatenate(
                [final[(q * band) // OY + r : (q * band) // OY + r + 1, :] for q in range(T)], axis=0
            )
        )
    for k in range(ks):
        index = source[:, 128 * k : 128 * k + 128]
        lanes_at = index & (OY - 1)
        row_at = (index // OY) & (rb - 1)
        value = None
        for r in range(rb):
            got = jnp.take_along_axis(operands[r], lanes_at, axis=1, mode="promise_in_bounds")
            value = got if value is None else jnp.where(row_at == r, got, value)
        for q in range(T):
            send_ref[q, AX + k : AX + k + 1, :] = value[q : q + 1, :]

    base = H * SENT + 2 * nbh * ks
    at = 8 * groups
    rims_left = left_side(at, at + AX + 2 * NP)
    rims_right = right_side(at, at + AX + 2 * NP)
    column_at = iota((AY, LEV), 0)

    def advance(i, before):
        at = i + 1
        return before + atmos_step * column_mean(
            mean_ref[at], rims_left[at : at + 1, :], rims_right[at : at + 1, :]
        )

    def tendency(i, row, others):
        along = [coef_ref[i + 1, m] * column_shift(row, s) for m, s in enumerate(SHIFTS)]
        across = [coef_ref[i + 1, len(SHIFTS) + m] * v for m, v in enumerate(others)]
        return sum_pairs(along + across)

    state = [advance(i, a_ref[i]) for i in range(AX)]
    rates = {}
    for i in range(AX):
        next_ref[i] = state[i]
        start = i - i % NP
        rates[i] = tendency(i, state[i], state[start : start + NP])
    for i, side, lo in ((-1, from_up, AX + 2), (AX, from_dn, AX + 1 + NP)):
        rim = advance(i, 0.0)
        edges = [
            (0.5 * atmos_step)
            * jnp.where(
                column_at == 0,
                rims_left[at : at + 1, :],
                jnp.where(column_at == AY - 1, rims_right[at : at + 1, :], 0.0),
            )
            for at in range(lo, lo + NP - 1)
        ]
        rates[i] = side(base + AY, base + 2 * AY) + tendency(i, rim, [rim] + edges)
    for i in range(AX):
        if i % NP == NP - 1:
            value = 0.5 * (rates[i] + rates[i + 1])
        elif i % NP == 0:
            value = 0.5 * (rates[i] + rates[i - 1])
        else:
            value = rates[i]
        mean2_ref[i] = value
    left_edge = mean2_ref[:, 0, :]
    right_edge = mean2_ref[:, AY - 1, :]
    for q in range(T):
        send_ref[q, :AX, :] = jnp.where(
            beside(T, 1) == q, right_edge, jnp.where(beside(T, -1) == q, left_edge, 0.0)
        )


def final_kernel(
    sizes, got_ref, next_ref, mean2_ref, h_ref, p_ref, tgt_ref, wgt_ref,
    a_dst, h_dst, p_dst, flux_dst, a_out, flux_out, sems,
):
    AX, AY, _, _, _, T, SLOT, _, _ = sizes
    copies = [
        pltpu.make_async_copy(source, target, sems.at[k])
        for k, (source, target) in enumerate(
            ((h_ref, h_dst), (p_ref, p_dst), (a_out, a_dst), (flux_out, flux_dst))
        )
    ]
    copies[0].start()
    copies[1].start()
    ks = SLOT // 128
    points = AX * AY // T
    left = got_ref[beside(T, -1), :AX, :]
    right = got_ref[beside(T, 1), :AX, :]
    for i in range(AX):
        a_out[i] = next_ref[i] + atmos_step * column_mean(
            mean2_ref[i], left[i : i + 1], right[i : i + 1]
        )
    copies[2].start()
    base = iota((T, 128), 0) * points
    totals = [jnp.zeros((T, 128), jnp.float32) for _ in range(points)]
    for k in range(ks):
        value = jnp.concatenate([got_ref[q, AX + k : AX + k + 1, :] for q in range(T)], axis=0)
        product = wgt_ref[:, 128 * k : 128 * k + 128] * value
        local = tgt_ref[:, 128 * k : 128 * k + 128] - base
        for m in range(points):
            totals[m] = totals[m] + jnp.where(local == m, product, 0.0)
    for m in range(points):
        flux_out[:, m : m + 1] = jnp.sum(totals[m], axis=1, keepdims=True)
    copies[3].start()
    for copy in copies:
        copy.wait()


def meeting(count, start):
    pairs = []
    for low in range(start, count + start, 2):
        pairs += [(low % count, (low + 1) % count), ((low + 1) % count, low % count)]
    return pairs


def on_device(C, T, *arguments):
    return step(C, T, *arguments)


def step(
    C, T,
    atmos_state, wind_field, ocean_height, ocean_potential, ocean_neighbors, ocean_coupling,
    downward_source, downward_target, downward_weight, upward_source, upward_target, upward_weight,
):
    AX, AY, LEV = atmos_state.shape
    OX, OY = ocean_height.shape
    SLOT = downward_source.shape[-1]
    H = SUBCYCLES
    n = AX * AY
    band = OX * OY // T
    nbh = H * OY // band
    ks = SLOT // 128
    sizes = (AX, AY, LEV, OX, OY, T, SLOT, H, nbh)
    f32, i32 = jnp.float32, jnp.int32
    static_rows = H * SENT + 2 * nbh * ks + 4 * AY + 8
    front_args = (
        downward_source, atmos_state, wind_field, ocean_neighbors, ocean_coupling,
        ocean_height, ocean_potential, downward_target, downward_weight,
    )
    front_outs = [
        ((C * T, 1, SLOT + 3 * n), f32), ((static_rows, 128), f32), ((static_rows, 128), f32),
        ((FIELDS - 4, OX, OY), f32), ((AX, AY, LEV), f32),
    ]
    slots, comp_first, comp_second, w8, rate = call(
        functools.partial(front_kernel, sizes, C),
        front_outs,
        front_args,
        scratch=[pltpu.VMEM(v.shape, v.dtype) for v in front_args]
        + [pltpu.VMEM(*v) for v in front_outs]
        + [pltpu.SemaphoreType.DMA((14,))],
        raw_in=True,
        raw_out=5,
        limit=None,
    )
    comp_second = lax.ppermute(comp_second, "comp", meeting(C, 1))
    comp_first = lax.ppermute(comp_first, "comp", meeting(C, 0))
    got = lax.all_to_all(slots, ("comp", "tile"), 0, 0, tiled=True)
    got = got.reshape(C * T, SLOT + 3 * n)

    edge_rows = OX + 2 * H + AX + 2 * NP
    NB = T + 2 * nbh
    ext, mean, left, right, high, low, weight, row, hot = call(
        functools.partial(prepare_kernel, sizes),
        [((FIELDS - 1, OX + 2 * H, OY), f32), ((AX + 2, AY, LEV), f32)]
        + [((edge_rows, 128), f32)] * 2
        + [((NB, SLOT), i32)] * 2
        + [((NB, SLOT), f32), ((NB, SLOT), i32), ((NB, 2 * H, SLOT), jnp.bfloat16)],
        (
            comp_first, comp_second, ocean_height, ocean_potential, w8,
            downward_target, downward_weight, rate,
        ),
    )
    tile_first, tile_second, part_hi, part_mid, part_lo = call(
        functools.partial(remap_kernel, sizes, C),
        [((edge_rows, 128), f32)] * 2 + [((NB, SLOT), f32)] * 3,
        (got, weight, row, hot, left, right),
        scratch=[pltpu.VMEM((OX + 2 * H, OY), f32)],
    )
    tile_second = lax.ppermute(tile_second, "tile", meeting(T, 1))
    tile_first = lax.ppermute(tile_first, "tile", meeting(T, 0))

    inner_h, inner_p, strips, coef = call(
        functools.partial(inner_kernel, sizes),
        [((OX, OY), f32)] * 2
        + [((FIELDS, OX + 2 * H, OY), f32), ((AX + 2, len(SHIFTS) + NP, AY, LEV), f32)],
        (ext, high, low, part_hi, part_mid, part_lo, comp_first, comp_second, wind_field),
        scratch=[pltpu.VMEM((OX + 2 * H, OY), f32), pltpu.VMEM((NB * band // LOW, OY), f32)],
    )
    height, potential, send, state, mean2 = call(
        functools.partial(ocean_kernel, sizes),
        [((OX, OY), f32)] * 2 + [((T, AX + max(8, ks), 128), f32)] + [((AX, AY, LEV), f32)] * 2,
        (
            strips, inner_h, inner_p, tile_first, tile_second, mean, comp_first, comp_second,
            atmos_state, coef, upward_source[0],
        ),
    )
    back = lax.all_to_all(send, "tile", 0, 0, tiled=True)
    atmos, height, potential, flux = call(
        functools.partial(final_kernel, sizes),
        [((AX, AY, LEV), f32)] + [((OX, OY), f32)] * 2 + [((T, n // T), f32)],
        (back, state, mean2, height, potential, upward_target[0], upward_weight[0]),
        scratch=[
            pltpu.VMEM((AX, AY, LEV), f32),
            pltpu.VMEM((T, n // T), f32),
            pltpu.SemaphoreType.DMA((4,)),
        ],
        raw_out=4,
    )
    return (atmos, height, potential, flux.reshape(AX, AY))


def solution(mesh):
    return jax.shard_map(
        functools.partial(on_device, mesh.shape["comp"], mesh.shape["tile"]),
        mesh=mesh,
        in_specs=(
            P("comp", "tile", None),
            P(None, "comp", "tile", None),
            P("comp", "tile"),
            P("comp", "tile"),
            P(None, "comp", "tile"),
            P(None, "comp", "tile"),
            P("comp", "tile", None),
            P("comp", "tile", None),
            P("comp", "tile", None),
            P("comp", "tile", None),
            P("comp", "tile", None),
            P("comp", "tile", None),
        ),
        out_specs=(
            P("comp", "tile", None),
            P("comp", "tile"),
            P("comp", "tile"),
            P("comp", "tile"),
        ),
        check_vma=False,
    )
```
